128 devices in a mesh: band: 8 (over x, core), mesh: 16 (over y, z).
Axes of the slice: x: 4, y: 4, z: 4, core: 2. Of those that a mesh axis runs over, the one named last changes fastest.
Arguments:
- grid_vars: bfloat16 [131072, 227], P(('band', 'mesh')), may hold values from -6 to 6
- mesh_latent: bfloat16 [40960, 512], P(('band', 'mesh')), may hold values from -6 to 6
- cotangent: bfloat16 [40960, 512], P(('band', 'mesh')), may hold values from -6 to 6
- edge_grid: int32 [524288], P(('band', 'mesh')), may hold values from 0 to 131071, as said below
- edge_mesh: int32 [524288], P(('band', 'mesh')), may hold values from 0 to 40959, as said below
- w_in: bfloat16 [227, 512], replicated, may hold values from -0.375 to 0.375
- b_in: float32 [512], replicated, may hold values from -4 to 4
- w_out: bfloat16 [512, 512], replicated, may hold values from -0.25 to 0.25
- norm_gain: float32 [512], replicated, may hold values from 0.1 to 1.9
- u_grid: bfloat16 [512, 512], replicated, may hold values from -0.25 to 0.25
- u_mesh: bfloat16 [512, 512], replicated, may hold values from -0.25 to 0.25
- b_edge: float32 [512], replicated, may hold values from -4 to 4
- w_edge: bfloat16 [512, 512], replicated, may hold values from -0.25 to 0.25
- w_self: bfloat16 [512, 512], replicated, may hold values from -0.25 to 0.25
- w_agg: bfloat16 [512, 512], replicated, may hold values from -0.1875 to 0.1875
- b_node: float32 [512], replicated, may hold values from -4 to 4
- w_node_out: bfloat16 [512, 512], replicated, may hold values from -0.25 to 0.25
Outputs:
- mesh_out: bfloat16 [40960, 512], P(('band', 'mesh'))
- grad_mesh: bfloat16 [40960, 512], P(('band', 'mesh'))
- grad_edge: float32 [512, 512], replicated
- grad_ugrid: float32 [512, 512], replicated
- grad_umesh: float32 [512, 512], replicated
The draws below stay inside these ranges and needn't reach their ends.
Inputs may be any that keep to these rules, and one draw needn't show every extreme that they name: `edge_grid`: the edges of one device (aligned blocks of 4096) have grid nodes among that device's 1024 grid nodes. `edge_mesh`: the edges of one device have mesh nodes among the 5120 mesh nodes of the device's band (the nodes of the 16 devices of that band), in nondecreasing order within the device's block. One device's edges reach at most 48 distinct mesh nodes owned by any one device (blocks of 320 mesh nodes); this most is reached in every draw.
All inputs are finite; a program needn't handle non-finite values.
Results may differ from the reference program's by a relative error of at most 0.013.
The reference program's roundings to bfloat16 on the way count: a program that leaves them out, or rounds other values in their place, can miss the bound.
Values may be sent and summed in bfloat16 or wider, within the bound.
A program may use at most 192 MiB of HBM per device.

```python
import jax
import jax.numpy as jnp
from jax import lax

D = 512
VARS = 227
GRID_DEV = 1024
EDGE_DEV = 4096
MESH_DEV = 320
CAP = 48
GRID = 131072
EDGES = 524288
MESH = 40960
BAND_NODES = 5120


def draw_edge_grid(key, part):
    devices = GRID // GRID_DEV
    local = jax.random.randint(jax.random.fold_in(key, 3), (devices, EDGE_DEV), 0, GRID_DEV)
    offset = jnp.arange(devices, dtype=jnp.int32)[:, None] * GRID_DEV
    return (local + offset).reshape(-1).astype(jnp.int32)


def draw_edge_mesh(key, part):
    devices = GRID // GRID_DEV
    owners = BAND_NODES // MESH_DEV
    bands = devices // owners
    keys = jax.random.split(jax.random.fold_in(key, 11), 4)
    band = jnp.arange(devices, dtype=jnp.int32) // owners
    middle = band == bands // 2
    upper = jnp.where(middle, CAP + 1, CAP * 3 // 4 + 1)
    counts = jax.random.randint(keys[0], (devices, owners), CAP // 2, upper[:, None])
    chosen = jax.random.randint(keys[1], (devices,), 0, owners)
    full = middle[:, None] & (jnp.arange(owners, dtype=jnp.int32)[None, :] == chosen[:, None])
    counts = jnp.where(full, CAP, counts)
    perm_keys = jax.random.split(keys[2], devices * owners)
    perms = jax.vmap(lambda k: jax.random.permutation(k, MESH_DEV))(perm_keys)
    perms = perms[:, :CAP].reshape(devices, owners, CAP).astype(jnp.int32)
    owner_base = jnp.arange(owners, dtype=jnp.int32)[None, :, None] * MESH_DEV
    candidates = (perms + owner_base).reshape(devices, owners * CAP)
    valid = (jnp.arange(CAP, dtype=jnp.int32)[None, None, :] < counts[:, :, None]).reshape(devices, owners * CAP)
    order = jnp.argsort(jnp.where(valid, 0, 1), axis=1, stable=True)
    touched = jnp.take_along_axis(candidates, order, axis=1)
    total = jnp.sum(counts, axis=1).astype(jnp.int32)
    picks = jax.random.randint(keys[3], (devices, EDGE_DEV), 0, 2 ** 30) % total[:, None]
    position = jnp.arange(EDGE_DEV, dtype=jnp.int32)[None, :]
    select = jnp.where(position < total[:, None], position, picks)
    nodes = jnp.sort(jnp.take_along_axis(touched, select, axis=1), axis=1)
    nodes = nodes + (band * BAND_NODES)[:, None]
    return nodes.reshape(-1).astype(jnp.int32)


def shard_levels(stream_key, shape, pieces, smallest, largest):
    def one(dim, shards_of):
        heights = jax.random.uniform(jax.random.fold_in(jax.random.fold_in(stream_key, 6), dim), (shards_of,), jnp.float32, smallest / len(pieces), largest / len(pieces))
        return jnp.repeat(jnp.exp(heights), shape[dim] // shards_of).reshape((-1,) + (1,) * (len(shape) - dim - 1))

    factor_of = one(*pieces[0])
    for cut in pieces[1:]:
        factor_of = factor_of * one(*cut)
    return factor_of


def noise(key, dims, scale, most, shards=(), kind=jnp.bfloat16):
    array = jax.random.normal(key, dims, jnp.float32) * scale
    if len(shards) > 0:
        array = shard_levels(key, dims, shards, -0.22, 0.18) * array
    return jnp.clip(array, min=-most, max=most).astype(kind)


def setup_inputs(seed: int = 0) -> dict:
    key_of = jax.random.split(jax.random.key(seed), 18)
    grid_vars = noise(key_of[0], (GRID, VARS), 1.0, 6.0, ((0, 128),))
    mesh_latent = noise(key_of[1], (MESH, D), 1.0, 6.0, ((0, 128),))
    cotangent = noise(key_of[2], (MESH, D), 1.0, 6.0, ((0, 128),))
    edge_grid = draw_edge_grid(jax.random.fold_in(key_of[17], 71), 0)
    edge_mesh = draw_edge_mesh(jax.random.fold_in(key_of[17], 71), 0)
    w_in = noise(key_of[5], (VARS, D), VARS ** -0.5, 0.375)
    b_in = noise(key_of[6], (D,), 1.0, 4.0, (), jnp.float32)
    w_out = noise(key_of[7], (D, D), D ** -0.5, 0.25)
    norm_gain = jnp.clip(1.0 + 0.18 * jax.random.normal(key_of[8], (D,), jnp.float32), 0.1, 1.9)
    u_grid = noise(key_of[9], (D, D), D ** -0.5, 0.25)
    u_mesh = noise(key_of[10], (D, D), D ** -0.5, 0.25)
    b_edge = noise(key_of[11], (D,), 1.0, 4.0, (), jnp.float32)
    w_edge = noise(key_of[12], (D, D), D ** -0.5, 0.25)
    w_self = noise(key_of[13], (D, D), D ** -0.5, 0.25)
    w_agg = noise(key_of[14], (D, D), (2 * D) ** -0.5, 0.1875)
    b_node = noise(key_of[15], (D,), 1.0, 4.0, (), jnp.float32)
    w_node_out = noise(key_of[16], (D, D), D ** -0.5, 0.25)
    return {"grid_vars": grid_vars, "mesh_latent": mesh_latent, "cotangent": cotangent, "edge_grid": edge_grid, "edge_mesh": edge_mesh, "w_in": w_in, "b_in": b_in, "w_out": w_out, "norm_gain": norm_gain, "u_grid": u_grid, "u_mesh": u_mesh, "b_edge": b_edge, "w_edge": w_edge, "w_self": w_self, "w_agg": w_agg, "b_node": b_node, "w_node_out": w_node_out}


def swish(v):
    return v * jax.nn.sigmoid(v)

def swish_grad(v):
    s = jax.nn.sigmoid(v)
    return s * (1.0 + v * (1.0 - s))

def layer_norm(v, gain):
    mean = lax.optimization_barrier(jnp.mean(v, axis=-1, keepdims=True))
    centred = v - mean
    var = lax.optimization_barrier(jnp.mean(centred * centred, axis=-1, keepdims=True))
    return centred * jax.lax.rsqrt(var + 1e-05) * gain

def mm(a, b):
    return jnp.dot(a, b, preferred_element_type=jnp.float32)

def reference(grid_vars, mesh_latent, cotangent, edge_grid, edge_mesh, w_in, b_in, w_out, norm_gain, u_grid, u_mesh, b_edge, w_edge, w_self, w_agg, b_node, w_node_out):
    hidden = swish(mm(grid_vars, w_in) + b_in).astype(jnp.bfloat16)
    latent = layer_norm(mm(hidden, w_out), norm_gain).astype(jnp.bfloat16)
    proj_grid = mm(latent, u_grid).astype(jnp.bfloat16)
    proj_mesh = mm(mesh_latent, u_mesh).astype(jnp.bfloat16)
    pre = proj_grid[edge_grid].astype(jnp.float32) + proj_mesh[edge_mesh].astype(jnp.float32) + b_edge
    act = swish(pre).astype(jnp.bfloat16)
    message = mm(act, w_edge).astype(jnp.bfloat16)
    agg = jax.ops.segment_sum(message.astype(jnp.float32), edge_mesh, num_segments=MESH).astype(jnp.bfloat16)
    node_pre = mm(mesh_latent, w_self) + mm(agg, w_agg) + b_node
    node_act = swish(node_pre).astype(jnp.bfloat16)
    mesh_out = (mesh_latent.astype(jnp.float32) + mm(node_act, w_node_out)).astype(jnp.bfloat16)
    g_node = (mm(cotangent, w_node_out.T) * swish_grad(node_pre)).astype(jnp.bfloat16)
    g_agg = mm(g_node, w_agg.T).astype(jnp.bfloat16)
    g_msg = g_agg[edge_mesh]
    scale = EDGES ** (-0.5)
    grad_edge = mm(act.T, g_msg) * scale
    g_edge = (mm(g_msg, w_edge.T) * swish_grad(pre)).astype(jnp.bfloat16)
    g_pgrid = jax.ops.segment_sum(g_edge.astype(jnp.float32), edge_grid, num_segments=GRID).astype(jnp.bfloat16)
    g_pmesh = jax.ops.segment_sum(g_edge.astype(jnp.float32), edge_mesh, num_segments=MESH).astype(jnp.bfloat16)
    grad_ugrid = mm(latent.T, g_pgrid) * scale
    grad_umesh = mm(mesh_latent.T, g_pmesh) * scale
    grad_mesh = (cotangent.astype(jnp.float32) + mm(g_node, w_self.T) + mm(g_pmesh, u_mesh.T)).astype(jnp.bfloat16)
    return (mesh_out, grad_mesh, grad_edge, grad_ugrid, grad_umesh)
```

```python
import functools

import jax
import jax.numpy as jnp
from jax import lax
from jax.experimental import pallas as pl
from jax.experimental.pallas import tpu as pltpu
from jax.sharding import PartitionSpec as P

CAP = 48
MESH = pl.DeviceIdType.MESH
F32 = jnp.float32
BF16 = jnp.bfloat16
VMEM_LIMIT = 60 * 1024 * 1024


def sigmoid(v):
    return 0.5 + 0.5 * jnp.tanh(0.5 * v)


def dot(a, b):
    return jnp.dot(a, b, preferred_element_type=F32)


def dot_nt(a, b):
    return lax.dot_general(a, b, (((1,), (1,)), ((), ())), preferred_element_type=F32)


def dot_tn(a, b):
    return lax.dot_general(a, b, (((0,), (0,)), ((), ())), preferred_element_type=F32)


def iota(shape, dim):
    return lax.broadcasted_iota(jnp.int32, shape, dim)


def onehot(mask):
    return jnp.where(mask, 1.0, 0.0).astype(BF16)


def enter(axes):
    barrier = pltpu.get_barrier_semaphore()
    total = 0
    for axis, n in axes:
        me = lax.axis_index(axis)
        for d in range(1, n):
            pl.semaphore_signal(
                barrier, inc=1, device_id={axis: lax.rem(me + d, n)}, device_id_type=MESH
            )
        total += n - 1
    pl.semaphore_wait(barrier, total)


def send_all(axis, n, src, dst, send_sem, recv_sem):
    me = lax.axis_index(axis)
    copies = []
    for d in range(1, n):
        peer = lax.rem(me + d, n)
        copy = pltpu.make_async_remote_copy(
            src_ref=src(peer),
            dst_ref=dst(me),
            send_sem=send_sem.at[d],
            recv_sem=recv_sem.at[d],
            device_id={axis: peer},
            device_id_type=MESH,
        )
        copy.start()
        copies.append(copy)
    return copies


def wait_all(copies):
    for copy in copies:
        copy.wait()


def columns(rows_ref, out_ref):
    rows = rows_ref.shape[0]
    values = rows_ref[...].astype(F32)
    pad = jnp.zeros((128 - rows, 128), F32)
    turned = jnp.transpose(jnp.concatenate([values, pad], axis=0))
    for r in range(rows):
        out_ref[r * 128 : (r + 1) * 128, :] = jnp.broadcast_to(
            turned[:, r : r + 1], (128, 128)
        ).astype(jnp.int32)


def fetch_kernel(
    nb, nm, em, eg, gv, ml, w_in, b_in, w_out, gain, u_grid, u_mesh,
    table, pick, latent, pgrid, slots, slot_col, grid_col,
    local_grid, left, right, ids_out, ids_in, asked, landed, pmesh, s1, r1, s2, r2,
):
    mesh_dev = ml.shape[0]
    grid_dev = gv.shape[0]
    rows = em.shape[0]
    me = lax.axis_index("mesh")
    band = lax.axis_index("band")
    enter((("mesh", nm),))
    x = em[...] - band * (nm * mesh_dev)
    lane = iota(x.shape, 1)
    row = iota(x.shape, 0)
    prev = pltpu.roll(x, 1, 1)
    prev = jnp.where(lane == 0, pltpu.roll(prev, 1, 0), prev)
    fresh = jnp.where((x != prev) | ((lane == 0) & (row == 0)), 1.0, 0.0)
    fb = fresh.astype(BF16)
    upper = onehot(iota((128, 128), 0) <= iota((128, 128), 1))
    totals = dot(fb, jnp.ones((128, 128), BF16)).astype(BF16)
    lower = onehot(iota((rows, rows), 1) < iota((rows, rows), 0))
    rank = dot(fb, upper) + dot(lower, totals) - 1.0
    owner = jnp.zeros(x.shape, jnp.int32)
    first = jnp.zeros(x.shape, F32)
    for o in range(1, nm):
        later = x >= o * mesh_dev
        begun = jnp.sum(jnp.where(later, 0.0, fresh), keepdims=True)
        owner = owner + jnp.where(later, 1, 0)
        first = jnp.where(later, begun, first)
    inner = (rank - first).astype(jnp.int32)
    slots[...] = owner * CAP + inner
    node = x - owner * mesh_dev
    high = jnp.right_shift(node, 4)
    low = node - high * 16
    high = jnp.where(fresh > 0, high, 0).astype(F32)
    low = jnp.where(fresh > 0, low, 0).astype(F32)
    owner_id = iota((nm, 128), 0)
    inner_id = iota((128, 128), 0)
    for r in range(rows):
        cut = slice(r * 128, (r + 1) * 128)
        mine = owner[r : r + 1, :] == owner_id
        left[0:nm, cut] = jnp.where(mine, high[r : r + 1, :], 0.0).astype(BF16)
        left[nm : 2 * nm, cut] = jnp.where(mine, low[r : r + 1, :], 0.0).astype(BF16)
        right[:, cut] = onehot(inner[r : r + 1, :] == inner_id)
    both = dot_nt(left[...], right[...])
    ids = both[0:nm] * 16.0 + both[nm : 2 * nm]
    for o in range(nm):
        ids_out[o] = jnp.broadcast_to(ids[o : o + 1, :], (8, 128))
    sent = send_all("mesh", nm, lambda p: ids_out.at[p], lambda q: ids_in.at[q], s1, r1)
    ids_in[me] = ids_out[me]
    pmesh[0:mesh_dev, :] = dot(ml[...], u_mesh[...]).astype(BF16)
    pmesh[mesh_dev:, :] = jnp.zeros((pmesh.shape[0] - mesh_dev, pmesh.shape[1]), BF16)
    columns(slots, slot_col)
    local_grid[...] = eg[...] - (band * nm + me) * grid_dev
    columns(local_grid, grid_col)
    wait_all(sent)
    turned = jnp.transpose(ids_in[...].reshape(nm * 8, 128))
    for q in range(nm):
        ids_q = jnp.broadcast_to(turned[0:CAP, q * 8 : q * 8 + 1], (CAP, 128)).astype(jnp.int32)
        for t in range(pick.shape[1] // 128):
            pick[q * CAP : (q + 1) * CAP, t * 128 : (t + 1) * 128] = onehot(
                ids_q == iota((CAP, 128), 1) + t * 128
            )
    asked[...] = dot(pick[...], pmesh[...]).astype(BF16).reshape(asked.shape)
    sent = send_all("mesh", nm, lambda p: asked.at[p], lambda q: landed.at[q], s2, r2)
    landed[me] = asked[me]
    step = 256

    def grid_rows(i, carry):
        cut = pl.ds(pl.multiple_of(i * step, step), step)
        v = dot(gv[cut, :], w_in[...]) + b_in[...]
        hidden = (v * sigmoid(v)).astype(BF16)
        y = dot(hidden, w_out[...])
        centred = y - jnp.mean(y, axis=-1, keepdims=True)
        var = jnp.mean(centred * centred, axis=-1, keepdims=True)
        lat = (centred * lax.rsqrt(var + 1e-05) * gain[...]).astype(BF16)
        latent[cut, :] = lat
        pgrid[cut, :] = dot(lat, u_grid[...]).astype(BF16)
        return carry

    lax.fori_loop(0, grid_dev // step, grid_rows, 0)
    wait_all(sent)
    table[...] = landed[...].reshape(table.shape)


EB = 512
TB = 256


def edge_kernel(slot_s, slots, grid_rows, slot_col, grid_col, table, pgrid, b_edge,
                a_out, s_out, slope, acc, pre, both):
    rows = slots.shape[0]
    width = table.shape[1]
    tiles = table.shape[0] // TB
    per = EB // 128
    acc[...] = jnp.zeros_like(acc)

    def block(b, carry):
        cut = pl.ds(pl.multiple_of(b * EB, EB), EB)
        gcol = grid_col[cut, :]
        hot = jnp.concatenate(
            [onehot(gcol == iota((EB, 128), 1) + t * 128) for t in range(pgrid.shape[0] // 128)],
            axis=1,
        )
        pre[...] = dot(hot, pgrid[...]) + b_edge[...]
        low = slot_s[b * per, 0]
        high = slot_s[b * per + per - 1, 127]
        for t in range(tiles):
            @pl.when((low < (t + 1) * TB) & (high >= t * TB))
            def _():
                scol = slot_col[cut, :]
                hot = jnp.concatenate(
                    [onehot(scol == iota((EB, 128), 1) + (t * TB + u * 128)) for u in range(TB // 128)],
                    axis=1,
                )
                pre[...] += dot(hot, table[t * TB : (t + 1) * TB, :])

        v = pre[...]
        s = sigmoid(v)
        act = v * s
        both[:, 0:width] = act.astype(BF16)
        sl = (s + act * (1.0 - s)).astype(BF16)
        both[:, width:] = sl
        slope[cut, :] = sl
        for t in range(tiles):
            @pl.when((low < (t + 1) * TB) & (high >= t * TB))
            def _():
                hot = jnp.concatenate(
                    [onehot(slots[pl.ds(b * per + u, 1), :] == iota((TB, 128), 0) + t * TB) for u in range(per)],
                    axis=1,
                )
                acc[t * TB : (t + 1) * TB, :] += dot(hot, both[...])

        return carry

    lax.fori_loop(0, rows // per, block, 0)
    a_out[...] = acc[:, 0:width].astype(BF16)
    s_out[...] = acc[:, width:].astype(BF16)


def node_kernel(
    nm, a_part, s_part, pick, ml, ct, w_edge, w_self, w_agg, b_node, w_node, u_mesh,
    mesh_out, grad_mesh, htable, g_edge, g_umesh,
    a_in, s_in, asked, landed, s1, r1, s2, r2, s3, r3,
):
    mesh_dev = ml.shape[0]
    me = lax.axis_index("mesh")
    enter((("mesh", nm),))
    sent_a = send_all("mesh", nm, lambda p: a_part.at[p], lambda q: a_in.at[q], s1, r1)
    sent_s = send_all("mesh", nm, lambda p: s_part.at[p], lambda q: s_in.at[q], s2, r2)
    a_in[me] = a_part[me]
    s_in[me] = s_part[me]
    flat = (a_in.shape[0] * a_in.shape[1], a_in.shape[2])
    own = dot(ml[...], w_self[...]) + b_node[...]
    back = dot_nt(ct[...], w_node[...])
    wait_all(sent_a)
    acts = dot_tn(pick[...], a_in[...].reshape(flat))[0:mesh_dev].astype(BF16)
    agg = dot(acts, w_edge[...]).astype(BF16)
    node_pre = own + dot(agg, w_agg[...])
    s = sigmoid(node_pre)
    node_act = node_pre * s
    g_node = (back * (s + node_act * (1.0 - s))).astype(BF16)
    g_agg = dot_nt(g_node, w_agg[...]).astype(BF16)
    h = dot_nt(g_agg, w_edge[...])
    hb = jnp.concatenate(
        [h.astype(BF16), jnp.zeros((pick.shape[1] - mesh_dev, h.shape[1]), BF16)], axis=0
    )
    asked[...] = dot(pick[...], hb).astype(BF16).reshape(asked.shape)
    sent_h = send_all("mesh", nm, lambda p: asked.at[p], lambda q: landed.at[q], s3, r3)
    landed[me] = asked[me]
    mesh_out[...] = (ml[...].astype(F32) + dot(node_act.astype(BF16), w_node[...])).astype(BF16)
    g_edge[...] = dot_tn(acts, g_agg).astype(BF16)
    part = ct[...].astype(F32) + dot_nt(g_node, w_self[...])
    wait_all(sent_s)
    slopes = dot_tn(pick[...], s_in[...].reshape(flat))[0:mesh_dev]
    g_pmesh = (h * slopes).astype(BF16)
    g_umesh[...] = dot_tn(ml[...], g_pmesh).astype(BF16)
    grad_mesh[...] = (part + dot_nt(g_pmesh, u_mesh[...])).astype(BF16)
    wait_all(sent_h)
    htable[...] = landed[...].reshape(htable.shape)


def grid_kernel(slot_s, grid_rows, slot_col, htable, slope, latent, g_ugrid, acc, pre):
    rows = grid_rows.shape[0]
    tiles = htable.shape[0] // TB
    per = EB // 128
    acc[...] = jnp.zeros_like(acc)

    def block(b, carry):
        cut = pl.ds(pl.multiple_of(b * EB, EB), EB)
        low = slot_s[b * per, 0]
        high = slot_s[b * per + per - 1, 127]
        pre[...] = jnp.zeros_like(pre)
        for t in range(tiles):
            @pl.when((low < (t + 1) * TB) & (high >= t * TB))
            def _():
                scol = slot_col[cut, :]
                hot = jnp.concatenate(
                    [onehot(scol == iota((EB, 128), 1) + (t * TB + u * 128)) for u in range(TB // 128)],
                    axis=1,
                )
                pre[...] += dot(hot, htable[t * TB : (t + 1) * TB, :])

        g = (pre[...] * slope[cut, :].astype(F32)).astype(BF16)
        n = acc.shape[0]
        hot = jnp.concatenate(
            [onehot(grid_rows[pl.ds(b * per + u, 1), :] == iota((n, 128), 0)) for u in range(per)],
            axis=1,
        )
        acc[...] += dot(hot, g)
        return carry

    lax.fori_loop(0, rows // per, block, 0)
    g_ugrid[...] = dot_tn(latent[...], acc[...].astype(BF16)).astype(BF16)


def reduce_kernel(nb, nm, scale, ge, gu, gg, oe, ou, og, *scratch):
    axes = {"band": nb, "mesh": nm}
    enter((("band", nb), ("mesh", nm)))
    width = ge.shape[1]
    plans = []
    for i, (src, out) in enumerate(((ge, oe), (gu, ou), (gg, og))):
        big, small = ("mesh", "band") if i == 2 else ("band", "mesh")
        plans.append((src, out, big, small) + tuple(scratch[i * 10 : (i + 1) * 10]))
    stage = []
    for src, out, big, small, in1, mid, in2, own, all2, all1, *sems in plans:
        n = axes[big]
        rows = in1.shape[1]
        stage.append(send_all(
            big, n,
            lambda p, src=src, rows=rows: src.at[pl.ds(pl.multiple_of(p * rows, 16), rows), :],
            lambda q, in1=in1: in1.at[q], sems[0].at[0], sems[0].at[1]))
        me = lax.axis_index(big)
        in1[me] = src[pl.ds(pl.multiple_of(me * rows, 16), rows), :]
    nxt = []
    for k, (src, out, big, small, in1, mid, in2, own, all2, all1, *sems) in enumerate(plans):
        wait_all(stage[k])
        n, m = axes[big], axes[small]
        total = in1[0].astype(F32)
        for q in range(1, n):
            total = total + in1[q].astype(F32)
        total = total.astype(BF16)
        pr, pc = mid.shape[1], mid.shape[2]
        cols = width // pc
        for i in range(m):
            a, c = i // cols, i % cols
            mid[i] = total[a * pr : (a + 1) * pr, c * pc : (c + 1) * pc]
        nxt.append(send_all(small, m, lambda p, mid=mid: mid.at[p], lambda q, in2=in2: in2.at[q],
                            sems[1].at[0], sems[1].at[1]))
        me = lax.axis_index(small)
        in2[me] = mid[me]
    stage, nxt = nxt, []
    for k, (src, out, big, small, in1, mid, in2, own, all2, all1, *sems) in enumerate(plans):
        wait_all(stage[k])
        m = axes[small]
        total = in2[0].astype(F32)
        for q in range(1, m):
            total = total + in2[q].astype(F32)
        own[...] = (total * scale).astype(BF16)
        nxt.append(send_all(small, m, lambda p, own=own: own, lambda q, all2=all2: all2.at[q],
                            sems[2].at[0], sems[2].at[1]))
        all2[lax.axis_index(small)] = own[...]
    stage, nxt = nxt, []
    for k, (src, out, big, small, in1, mid, in2, own, all2, all1, *sems) in enumerate(plans):
        wait_all(stage[k])
        n, m = axes[big], axes[small]
        pr, pc = mid.shape[1], mid.shape[2]
        cols = width // pc
        me = lax.axis_index(big)
        for i in range(m):
            a, c = i // cols, i % cols
            all1[me, a * pr : (a + 1) * pr, c * pc : (c + 1) * pc] = all2[i]
        nxt.append(send_all(big, n, lambda p, all1=all1, me=me: all1.at[me], lambda q, all1=all1: all1.at[q],
                            sems[3].at[0], sems[3].at[1]))
    for k, (src, out, big, small, in1, mid, in2, own, all2, all1, *sems) in enumerate(plans):
        wait_all(nxt[k])
        out[...] = all1[...].reshape(out.shape).astype(F32)


def vmem():
    return pl.BlockSpec(memory_space=pltpu.VMEM)


def shape(dims, kind):
    return jax.ShapeDtypeStruct(dims, kind)


def params(cid=None):
    if cid is None:
        return pltpu.CompilerParams(vmem_limit_bytes=VMEM_LIMIT)
    return pltpu.CompilerParams(
        vmem_limit_bytes=VMEM_LIMIT, collective_id=cid, has_side_effects=True
    )


def shards(
    nb, nm, grid_vars, mesh_latent, cotangent, edge_grid, edge_mesh, w_in, b_in, w_out, norm_gain,
    u_grid, u_mesh, b_edge, w_edge, w_self, w_agg, b_node, w_node_out,
):
    grid_dev = grid_vars.shape[0]
    mesh_dev, width = mesh_latent.shape
    edges = edge_grid.shape[0]
    rows = edges // 128
    slots_n = nm * CAP
    padded = -(-mesh_dev // 128) * 128
    sem = pltpu.SemaphoreType.DMA
    em = edge_mesh.reshape(rows, 128)
    eg = edge_grid.reshape(rows, 128)
    table, pick, latent, pgrid, slots, slot_col, grid_col, local_grid = pl.pallas_call(
        functools.partial(fetch_kernel, nb, nm),
        out_shape=(
            shape((slots_n, width), BF16), shape((slots_n, padded), BF16),
            shape((grid_dev, width), BF16), shape((grid_dev, width), BF16),
            shape((rows, 128), jnp.int32), shape((edges, 128), jnp.int32),
            shape((edges, 128), jnp.int32), shape((rows, 128), jnp.int32),
        ),
        in_specs=[vmem()] * 10,
        out_specs=(vmem(),) * 8,
        scratch_shapes=[
            pltpu.VMEM((2 * nm, edges), BF16), pltpu.VMEM((128, edges), BF16),
            pltpu.VMEM((nm, 8, 128), F32), pltpu.VMEM((nm, 8, 128), F32),
            pltpu.VMEM((nm, CAP, width), BF16), pltpu.VMEM((nm, CAP, width), BF16),
            pltpu.VMEM((padded, width), BF16),
            sem((nm,)), sem((nm,)), sem((nm,)), sem((nm,)),
        ],
        compiler_params=params(0),
        name="fetch",
    )(em, eg, grid_vars, mesh_latent, w_in, b_in.reshape(1, -1), w_out, norm_gain.reshape(1, -1),
      u_grid, u_mesh)
    a_part, s_part, slope = pl.pallas_call(
        edge_kernel,
        out_shape=(shape((slots_n, width), BF16), shape((slots_n, width), BF16), shape((edges, width), BF16)),
        in_specs=[pl.BlockSpec(memory_space=pltpu.SMEM)] + [vmem()] * 7,
        out_specs=(vmem(),) * 3,
        scratch_shapes=[
            pltpu.VMEM((slots_n, 2 * width), F32), pltpu.VMEM((EB, width), F32),
            pltpu.VMEM((EB, 2 * width), BF16),
        ],
        compiler_params=params(),
        name="edges",
    )(slots, slots, local_grid, slot_col, grid_col, table, pgrid, b_edge.reshape(1, -1))
    mesh_out, grad_mesh, htable, g_edge, g_umesh = pl.pallas_call(
        functools.partial(node_kernel, nm),
        out_shape=(
            shape((mesh_dev, width), BF16), shape((mesh_dev, width), BF16), shape((slots_n, width), BF16),
            shape((width, width), BF16), shape((width, width), BF16),
        ),
        in_specs=[vmem()] * 11,
        out_specs=(vmem(),) * 5,
        scratch_shapes=[pltpu.VMEM((nm, CAP, width), BF16)] * 4 + [sem((nm,))] * 6,
        compiler_params=params(1),
        name="nodes",
    )(a_part.reshape(nm, CAP, width), s_part.reshape(nm, CAP, width), pick, mesh_latent, cotangent,
      w_edge, w_self, w_agg, b_node.reshape(1, -1), w_node_out, u_mesh)
    g_ugrid = pl.pallas_call(
        grid_kernel,
        out_shape=shape((width, width), BF16),
        in_specs=[pl.BlockSpec(memory_space=pltpu.SMEM)] + [vmem()] * 5,
        out_specs=vmem(),
        scratch_shapes=[pltpu.VMEM((grid_dev, width), F32), pltpu.VMEM((EB, width), F32)],
        compiler_params=params(),
        name="grids",
    )(slots, local_grid, slot_col, htable, slope, latent)
    scratch = []
    for i in range(3):
        n, m = (nm, nb) if i == 2 else (nb, nm)
        big = width // n
        pc = min(4, m)
        piece = (big // (m // pc), width // pc)
        scratch += [
            pltpu.VMEM((n, big, width), BF16), pltpu.VMEM((m,) + piece, BF16),
            pltpu.VMEM((m,) + piece, BF16), pltpu.VMEM(piece, BF16), pltpu.VMEM((m,) + piece, BF16),
            pltpu.VMEM((n, big, width), BF16),
            sem((2, n)), sem((2, m)), sem((2, m)), sem((2, n)),
        ]
    scale = (edges * nb * nm) ** (-0.5)
    out = shape((width, width), F32)
    grad_edge, grad_umesh, grad_ugrid = pl.pallas_call(
        functools.partial(reduce_kernel, nb, nm, scale),
        out_shape=(out, out, out),
        in_specs=[vmem()] * 3,
        out_specs=(vmem(),) * 3,
        scratch_shapes=scratch,
        compiler_params=params(2),
        name="reduce",
    )(g_edge, g_umesh, g_ugrid)
    return (mesh_out, grad_mesh, grad_edge, grad_ugrid, grad_umesh)


def solution(mesh):
    split = P(("band", "mesh"), None)
    flat = P(("band", "mesh"))
    return jax.shard_map(
        functools.partial(shards, mesh.shape["band"], mesh.shape["mesh"]),
        mesh=mesh,
        in_specs=(split, split, split, flat, flat) + (P(),) * 12,
        out_specs=(split, split, P(), P(), P()),
        check_vma=False,
    )
```

```python
import functools

import jax
import jax.numpy as jnp
from jax import lax
from jax.experimental import pallas as pl
from jax.experimental.pallas import tpu as pltpu
from jax.sharding import PartitionSpec as P

CAP = 48
MESH = pl.DeviceIdType.MESH
F32 = jnp.float32
BF16 = jnp.bfloat16
VMEM_LIMIT = 60 * 1024 * 1024


def sigmoid(v):
    return 0.5 + 0.5 * jnp.tanh(0.5 * v)


def dot(a, b):
    return jnp.dot(a, b, preferred_element_type=F32)


def dot_nt(a, b):
    return lax.dot_general(a, b, (((1,), (1,)), ((), ())), preferred_element_type=F32)


def dot_tn(a, b):
    return lax.dot_general(a, b, (((0,), (0,)), ((), ())), preferred_element_type=F32)


def iota(shape, dim):
    return lax.broadcasted_iota(jnp.int32, shape, dim)


def onehot(mask):
    return jnp.where(mask, 1.0, 0.0).astype(BF16)


def enter(axes):
    barrier = pltpu.get_barrier_semaphore()
    total = 0
    for axis, n in axes:
        me = lax.axis_index(axis)
        for d in range(1, n):
            pl.semaphore_signal(
                barrier, inc=1, device_id={axis: lax.rem(me + d, n)}, device_id_type=MESH
            )
        total += n - 1
    pl.semaphore_wait(barrier, total)


def send_all(axis, n, src, dst, send_sem, recv_sem):
    me = lax.axis_index(axis)
    copies = []
    for d in range(1, n):
        peer = lax.rem(me + d, n)
        copy = pltpu.make_async_remote_copy(
            src_ref=src(peer),
            dst_ref=dst(me),
            send_sem=send_sem.at[d],
            recv_sem=recv_sem.at[d],
            device_id={axis: peer},
            device_id_type=MESH,
        )
        copy.start()
        copies.append(copy)
    return copies


def wait_all(copies):
    for copy in copies:
        copy.wait()


def columns(rows_ref, out_ref):
    rows = rows_ref.shape[0]
    values = rows_ref[...].astype(F32)
    pad = jnp.zeros((128 - rows, 128), F32)
    turned = jnp.transpose(jnp.concatenate([values, pad], axis=0))
    for r in range(rows):
        out_ref[r * 128 : (r + 1) * 128, :] = jnp.broadcast_to(
            turned[:, r : r + 1], (128, 128)
        ).astype(jnp.int32)


def fetch_kernel(
    nb, nm, em, eg, gv, ml, w_in, b_in, w_out, gain, u_grid, u_mesh,
    table, pick, latent, pgrid, slots, slot_col, grid_col,
    local_grid, left, right, ids_out, ids_in, asked, landed, pmesh, s1, r1, s2, r2,
):
    mesh_dev = ml.shape[0]
    grid_dev = gv.shape[1]
    rows = em.shape[0]
    me = lax.axis_index("mesh")
    band = lax.axis_index("band")
    enter((("mesh", nm),))
    x = em[...] - band * (nm * mesh_dev)
    lane = iota(x.shape, 1)
    row = iota(x.shape, 0)
    prev = pltpu.roll(x, 1, 1)
    prev = jnp.where(lane == 0, pltpu.roll(prev, 1, 0), prev)
    fresh = jnp.where((x != prev) | ((lane == 0) & (row == 0)), 1.0, 0.0)
    fb = fresh.astype(BF16)
    upper = onehot(iota((128, 128), 0) <= iota((128, 128), 1))
    totals = dot(fb, jnp.ones((128, 128), BF16)).astype(BF16)
    lower = onehot(iota((rows, rows), 1) < iota((rows, rows), 0))
    rank = dot(fb, upper) + dot(lower, totals) - 1.0
    owner = jnp.zeros(x.shape, jnp.int32)
    first = jnp.zeros(x.shape, F32)
    for o in range(1, nm):
        later = x >= o * mesh_dev
        begun = jnp.sum(jnp.where(later, 0.0, fresh), keepdims=True)
        owner = owner + jnp.where(later, 1, 0)
        first = jnp.where(later, begun, first)
    inner = (rank - first).astype(jnp.int32)
    slots[...] = owner * CAP + inner
    node = x - owner * mesh_dev
    high = jnp.right_shift(node, 4)
    low = node - high * 16
    high = jnp.where(fresh > 0, high, 0).astype(F32)
    low = jnp.where(fresh > 0, low, 0).astype(F32)
    owner_id = iota((nm, 128), 0)
    inner_id = iota((128, 128), 0)
    for r in range(rows):
        cut = slice(r * 128, (r + 1) * 128)
        mine = owner[r : r + 1, :] == owner_id
        left[0:nm, cut] = jnp.where(mine, high[r : r + 1, :], 0.0).astype(BF16)
        left[nm : 2 * nm, cut] = jnp.where(mine, low[r : r + 1, :], 0.0).astype(BF16)
        right[:, cut] = onehot(inner[r : r + 1, :] == inner_id)
    both = dot_nt(left[...], right[...])
    ids = both[0:nm] * 16.0 + both[nm : 2 * nm]
    for o in range(nm):
        ids_out[o] = jnp.broadcast_to(ids[o : o + 1, :], (8, 128))
    sent = send_all("mesh", nm, lambda p: ids_out.at[p], lambda q: ids_in.at[q], s1, r1)
    ids_in[me] = ids_out[me]
    pmesh[0:mesh_dev, :] = dot(ml[...], u_mesh[...]).astype(BF16)
    pmesh[mesh_dev:, :] = jnp.zeros((pmesh.shape[0] - mesh_dev, pmesh.shape[1]), BF16)
    columns(slots, slot_col)
    local_grid[...] = eg[...] - (band * nm + me) * grid_dev
    columns(local_grid, grid_col)
    wait_all(sent)
    turned = jnp.transpose(ids_in[...].reshape(nm * 8, 128))
    for q in range(nm):
        ids_q = jnp.broadcast_to(turned[0:CAP, q * 8 : q * 8 + 1], (CAP, 128)).astype(jnp.int32)
        for t in range(pick.shape[1] // 128):
            pick[q * CAP : (q + 1) * CAP, t * 128 : (t + 1) * 128] = onehot(
                ids_q == iota((CAP, 128), 1) + t * 128
            )
    asked[...] = dot(pick[...], pmesh[...]).astype(BF16).reshape(asked.shape)
    sent = send_all("mesh", nm, lambda p: asked.at[p], lambda q: landed.at[q], s2, r2)
    landed[me] = asked[me]
    step = 256

    def grid_rows(i, carry):
        cut = pl.ds(pl.multiple_of(i * step, step), step)
        v = dot_tn(gv[:, cut], w_in[...]) + b_in[...]
        hidden = (v * sigmoid(v)).astype(BF16)
        y = dot(hidden, w_out[...])
        centred = y - jnp.mean(y, axis=-1, keepdims=True)
        var = jnp.mean(centred * centred, axis=-1, keepdims=True)
        lat = (centred * lax.rsqrt(var + 1e-05) * gain[...]).astype(BF16)
        latent[cut, :] = lat
        pgrid[cut, :] = dot(lat, u_grid[...]).astype(BF16)
        return carry

    lax.fori_loop(0, grid_dev // step, grid_rows, 0)
    wait_all(sent)
    table[...] = landed[...].reshape(table.shape)


EB = 512
TB = 256


def edge_kernel(slot_s, slots, grid_rows, slot_col, grid_col, table, pgrid, b_edge,
                a_out, s_out, slope, acc, pre, both):
    rows = slots.shape[0]
    width = table.shape[1]
    tiles = table.shape[0] // TB
    per = EB // 128
    acc[...] = jnp.zeros_like(acc)

    def block(b, carry):
        cut = pl.ds(pl.multiple_of(b * EB, EB), EB)
        gcol = grid_col[cut, :]
        hot = jnp.concatenate(
            [onehot(gcol == iota((EB, 128), 1) + t * 128) for t in range(pgrid.shape[0] // 128)],
            axis=1,
        )
        pre[...] = dot(hot, pgrid[...]) + b_edge[...]
        low = slot_s[b * per, 0]
        high = slot_s[b * per + per - 1, 127]
        for t in range(tiles):
            @pl.when((low < (t + 1) * TB) & (high >= t * TB))
            def _():
                scol = slot_col[cut, :]
                hot = jnp.concatenate(
                    [onehot(scol == iota((EB, 128), 1) + (t * TB + u * 128)) for u in range(TB // 128)],
                    axis=1,
                )
                pre[...] += dot(hot, table[t * TB : (t + 1) * TB, :])

        v = pre[...]
        s = sigmoid(v)
        act = v * s
        both[:, 0:width] = act.astype(BF16)
        sl = (s + act * (1.0 - s)).astype(BF16)
        both[:, width:] = sl
        slope[cut, :] = sl
        for t in range(tiles):
            @pl.when((low < (t + 1) * TB) & (high >= t * TB))
            def _():
                hot = jnp.concatenate(
                    [onehot(slots[pl.ds(b * per + u, 1), :] == iota((TB, 128), 0) + t * TB) for u in range(per)],
                    axis=1,
                )
                acc[t * TB : (t + 1) * TB, :] += dot(hot, both[...])

        return carry

    lax.fori_loop(0, rows // per, block, 0)
    a_out[...] = acc[:, 0:width].astype(BF16)
    half = width // 2
    for c in range(2):
        s_out[c] = acc[:, width + c * half : width + (c + 1) * half].astype(BF16)


def make_sum(axes, scale, big, small, width, in1, mid, in2, own, all2, all1, q1, q2, q3, q4):
    n, m = axes[big], axes[small]
    rows = in1.shape[1]
    pr, pc = mid.shape[1], mid.shape[2]
    cols = width // pc
    live = {}

    def start(src):
        def part(p):
            return src.at[pl.ds(pl.multiple_of(p * rows, 16), rows), :]

        live[1] = send_all(big, n, part, lambda q: in1.at[q], q1.at[0], q1.at[1])
        me = lax.axis_index(big)
        in1[me] = src[pl.ds(pl.multiple_of(me * rows, 16), rows), :]

    def middle():
        wait_all(live[1])
        total = in1[0].astype(F32)
        for q in range(1, n):
            total = total + in1[q].astype(F32)
        for i in range(m):
            a, c = i // cols, i % cols
            mid[i] = total[a * pr : (a + 1) * pr, c * pc : (c + 1) * pc]
        live[2] = send_all(small, m, lambda p: mid.at[p], lambda q: in2.at[q], q2.at[0], q2.at[1])
        me = lax.axis_index(small)
        in2[me] = mid[me]

    def gather():
        wait_all(live[2])
        total = in2[0]
        for q in range(1, m):
            total = total + in2[q]
        own[...] = total * scale
        live[3] = send_all(small, m, lambda p: own, lambda q: all2.at[q], q3.at[0], q3.at[1])
        all2[lax.axis_index(small)] = own[...]

    def spread():
        wait_all(live[3])
        me = lax.axis_index(big)
        bands = []
        for a in range(m // cols):
            bands.append(jnp.concatenate([all2[a * cols + c] for c in range(cols)], axis=1))
        all1[me] = jnp.concatenate(bands, axis=0).astype(BF16)
        live[4] = send_all(big, n, lambda p: all1.at[me], lambda q: all1.at[q], q4.at[0], q4.at[1])

    def finish(out):
        wait_all(live[4])
        out[...] = all1[...].reshape(out.shape)

    return start, middle, gather, spread, finish


GB = 1024


def back_kernel(
    nb, nm, scale, pick, ml, ct, b_node, grid_rows, a_part, s_part, w_edge_h, w_self_h, w_agg_h,
    w_node_h, u_mesh_h, slot_col_h, slope_h, latent_h,
    mesh_out, grad_mesh, oe, ou, o0, o1,
    w_edge, w_self, w_agg, w_node, u_mesh, slot_col, slope, latent, load_sem, self_sem,
    a_in, s_in, asked, landed, hot_s, hot_g, acc, ge, gu, g0, g1,
    sa, ra, ss, rs, sh, rh, *sums,
):
    mesh_dev, width = ml.shape
    half = width // 2
    rows = grid_rows.shape[0]
    me = lax.axis_index("mesh")
    axes = {"band": nb, "mesh": nm}
    plans = [
        make_sum(axes, scale, big, small, w, *sums[i * 10 : (i + 1) * 10])
        for i, (big, small, w) in enumerate(
            (("band", "mesh", width), ("band", "mesh", width), ("mesh", "band", half), ("mesh", "band", half))
        )
    ]
    enter((("mesh", nm), ("band", nb)))
    sent_a = send_all("mesh", nm, lambda p: a_part.at[p], lambda q: a_in.at[q], sa, ra)
    own_a = pltpu.make_async_copy(a_part.at[me], a_in.at[me], self_sem.at[0])
    own_a.start()
    loads = []
    for i, (src, dst) in enumerate(
        ((w_self_h, w_self), (w_node_h, w_node), (slot_col_h, slot_col), (w_edge_h, w_edge), (w_agg_h, w_agg),
         (u_mesh_h, u_mesh), (slope_h, slope), (latent_h, latent))
    ):
        copy = pltpu.make_async_copy(src, dst, load_sem.at[i])
        copy.start()
        loads.append(copy)
    sent_s, own_s = [], []
    for c in range(2):
        if c == 0:
            sent_s.append(send_all("mesh", nm, lambda p: s_part.at[0, p], lambda q: s_in.at[0, q], ss.at[0], rs.at[0]))
        copy = pltpu.make_async_copy(s_part.at[c, me], s_in.at[c, me], self_sem.at[1 + c])
        copy.start()
        own_s.append(copy)
    loads[0].wait()
    own = dot(ml[...], w_self[...]) + b_node[...]
    loads[1].wait()
    back = dot_nt(ct[...], w_node[...])
    loads[2].wait()
    slots_n = hot_s.shape[1]
    grid_dev = hot_g.shape[0]

    def build(r, carry):
        cut = pl.ds(pl.multiple_of(r * 128, 128), 128)
        scol = slot_col[cut, :]
        for t in range(slots_n // 128):
            hot_s[cut, t * 128 : (t + 1) * 128] = onehot(scol == iota((128, 128), 1) + t * 128)
        hot_g[:, cut] = onehot(grid_rows[pl.ds(r, 1), :] == iota((grid_dev, 128), 0))
        return carry

    lax.fori_loop(0, rows, build, 0)
    for copy in loads[3:5]:
        copy.wait()
    own_a.wait()
    wait_all(sent_a)
    flat = nm * CAP
    acts = dot_tn(pick[...], a_in[...].reshape(flat, width))[0:mesh_dev].astype(BF16)
    agg = dot(acts, w_edge[...]).astype(BF16)
    node_pre = own + dot(agg, w_agg[...])
    s = sigmoid(node_pre)
    node_act = node_pre * s
    g_node = (back * (s + node_act * (1.0 - s))).astype(BF16)
    g_agg = dot_nt(g_node, w_agg[...]).astype(BF16)
    h = dot_nt(g_agg, w_edge[...])
    hb = jnp.concatenate(
        [h.astype(BF16), jnp.zeros((pick.shape[1] - mesh_dev, width), BF16)], axis=0
    )
    sent_h = []
    for c in range(2):
        asked[c] = dot(pick[...], hb[:, c * half : (c + 1) * half]).astype(BF16).reshape(nm, CAP, half)
        sent_h.append(send_all("mesh", nm, lambda p, c=c: asked.at[c, p], lambda q, c=c: landed.at[c, q],
                               sh.at[c], rh.at[c]))
        landed[c, me] = asked[c, me]
    sent_s.append(send_all("mesh", nm, lambda p: s_part.at[1, p], lambda q: s_in.at[1, q], ss.at[1], rs.at[1]))
    ge[...] = dot_tn(acts, g_agg).astype(BF16)
    plans[0][0](ge)
    mesh_out[...] = (ml[...].astype(F32) + dot(node_act.astype(BF16), w_node[...])).astype(BF16)
    part = ct[...].astype(F32) + dot_nt(g_node, w_self[...])
    for copy in loads[5:]:
        copy.wait()

    def grid_half(c):
        acc[...] = jnp.zeros_like(acc)
        col = slice(c * half, (c + 1) * half)
        table = landed[c].reshape(flat, half)

        def block(b, carry):
            cut = pl.ds(pl.multiple_of(b * GB, GB), GB)
            g = (dot(hot_s[cut, :], table) * slope[cut, col].astype(F32)).astype(BF16)
            acc[...] += dot(hot_g[:, cut], g)
            return carry

        lax.fori_loop(0, rows * 128 // GB, block, 0)
        return dot_tn(latent[...], acc[...].astype(BF16)).astype(BF16)

    wait_all(sent_h[0])
    g0[...] = grid_half(0)
    plans[2][0](g0)
    wait_all(sent_h[1])
    plans[0][1]()
    g1[...] = grid_half(1)
    plans[3][0](g1)
    for copy in own_s:
        copy.wait()
    wait_all(sent_s[0])
    wait_all(sent_s[1])
    slopes = jnp.concatenate(
        [dot_tn(pick[...], s_in[c].reshape(flat, half))[0:mesh_dev] for c in range(2)], axis=1
    )
    g_pmesh = (h * slopes).astype(BF16)
    gu[...] = dot_tn(ml[...], g_pmesh).astype(BF16)
    plans[1][0](gu)
    grad_mesh[...] = (part + dot_nt(g_pmesh, u_mesh[...])).astype(BF16)
    plans[2][1]()
    plans[0][2]()
    plans[3][1]()
    plans[1][1]()
    plans[2][2]()
    plans[0][3]()
    plans[3][2]()
    plans[1][2]()
    plans[2][3]()
    plans[3][3]()
    plans[1][3]()
    plans[0][4](oe)
    plans[2][4](o0)
    plans[3][4](o1)
    plans[1][4](ou)


def write_kernel(mo, gm, e, u, g0, g1, mo_out, gm_out, e_out, g_out, u_out):
    half = g0.shape[1]
    mo_out[...] = mo[...]
    gm_out[...] = gm[...]
    e_out[...] = e[...].astype(F32)
    u_out[...] = u[...].astype(F32)
    g_out[:, 0:half] = g0[...].astype(F32)
    g_out[:, half:] = g1[...].astype(F32)


def vmem():
    return pl.BlockSpec(memory_space=pltpu.VMEM)


def shape(dims, kind):
    return jax.ShapeDtypeStruct(dims, kind)


def params(cid=None):
    if cid is None:
        return pltpu.CompilerParams(vmem_limit_bytes=VMEM_LIMIT)
    return pltpu.CompilerParams(
        vmem_limit_bytes=VMEM_LIMIT, collective_id=cid, has_side_effects=True
    )


def shards(
    nb, nm, grid_vars, mesh_latent, cotangent, edge_grid, edge_mesh, w_in, b_in, w_out, norm_gain,
    u_grid, u_mesh, b_edge, w_edge, w_self, w_agg, b_node, w_node_out,
):
    grid_dev = grid_vars.shape[0]
    mesh_dev, width = mesh_latent.shape
    edges = edge_grid.shape[0]
    rows = edges // 128
    slots_n = nm * CAP
    padded = -(-mesh_dev // 128) * 128
    sem = pltpu.SemaphoreType.DMA
    em = edge_mesh.reshape(rows, 128)
    eg = edge_grid.reshape(rows, 128)
    table, pick, latent, pgrid, slots, slot_col, grid_col, local_grid = pl.pallas_call(
        functools.partial(fetch_kernel, nb, nm),
        out_shape=(
            shape((slots_n, width), BF16), shape((slots_n, padded), BF16),
            shape((grid_dev, width), BF16), shape((grid_dev, width), BF16),
            shape((rows, 128), jnp.int32), shape((edges, 128), jnp.int32),
            shape((edges, 128), jnp.int32), shape((rows, 128), jnp.int32),
        ),
        in_specs=[vmem()] * 10,
        out_specs=(vmem(),) * 8,
        scratch_shapes=[
            pltpu.VMEM((2 * nm, edges), BF16), pltpu.VMEM((128, edges), BF16),
            pltpu.VMEM((nm, 8, 128), F32), pltpu.VMEM((nm, 8, 128), F32),
            pltpu.VMEM((nm, CAP, width), BF16), pltpu.VMEM((nm, CAP, width), BF16),
            pltpu.VMEM((padded, width), BF16),
            sem((nm,)), sem((nm,)), sem((nm,)), sem((nm,)),
        ],
        compiler_params=params(0),
        name="fetch",
    )(em, eg, grid_vars.T, mesh_latent, w_in, b_in.reshape(1, -1), w_out, norm_gain.reshape(1, -1),
      u_grid, u_mesh)
    a_part, s_part, slope = pl.pallas_call(
        edge_kernel,
        out_shape=(
            shape((slots_n, width), BF16), shape((2, slots_n, width // 2), BF16), shape((edges, width), BF16),
        ),
        in_specs=[pl.BlockSpec(memory_space=pltpu.SMEM)] + [vmem()] * 7,
        out_specs=(vmem(),) * 3,
        scratch_shapes=[
            pltpu.VMEM((slots_n, 2 * width), F32), pltpu.VMEM((EB, width), F32),
            pltpu.VMEM((EB, 2 * width), BF16),
        ],
        compiler_params=params(),
        name="edges",
    )(slots, slots, local_grid, slot_col, grid_col, table, pgrid, b_edge.reshape(1, -1))
    half = width // 2
    sums = []
    for n, m, w in ((nb, nm, width), (nb, nm, width), (nm, nb, half), (nm, nb, half)):
        big = width // n
        across = min(m, w // 128)
        piece = (big // (m // across), w // across)
        sums += [
            pltpu.VMEM((n, big, w), BF16), pltpu.VMEM((m,) + piece, F32),
            pltpu.VMEM((m,) + piece, F32), pltpu.VMEM(piece, F32), pltpu.VMEM((m,) + piece, F32),
            pltpu.VMEM((n, big, w), BF16),
            sem((2, n)), sem((2, m)), sem((2, m)), sem((2, n)),
        ]
    scale = (edges * nb * nm) ** (-0.5)
    node = shape((mesh_dev, width), BF16)
    square = shape((width, width), BF16)
    slim = shape((width, half), BF16)
    matrix = pltpu.VMEM((width, width), BF16)
    outs = pl.pallas_call(
        functools.partial(back_kernel, nb, nm, scale),
        out_shape=(node, node, square, square, slim, slim),
        in_specs=[vmem()] * 5 + [pl.BlockSpec(memory_space=pl.ANY)] * 10,
        out_specs=(vmem(),) * 6,
        scratch_shapes=[matrix] * 5 + [
            pltpu.VMEM((edges, 128), jnp.int32), pltpu.VMEM((edges, width), BF16),
            pltpu.VMEM((grid_dev, width), BF16), sem((8,)), sem((3,)),
            pltpu.VMEM((nm, CAP, width), BF16), pltpu.VMEM((2, nm, CAP, half), BF16),
            pltpu.VMEM((2, nm, CAP, half), BF16), pltpu.VMEM((2, nm, CAP, half), BF16),
            pltpu.VMEM((edges, slots_n), BF16), pltpu.VMEM((grid_dev, edges), BF16),
            pltpu.VMEM((grid_dev, half), F32), matrix, matrix,
            pltpu.VMEM((width, half), BF16), pltpu.VMEM((width, half), BF16),
            sem((nm,)), sem((nm,)), sem((2, nm)), sem((2, nm)), sem((2, nm)), sem((2, nm)),
        ] + sums,
        compiler_params=params(1),
        name="back",
    )(pick, mesh_latent, cotangent, b_node.reshape(1, -1), local_grid, a_part.reshape(nm, CAP, width),
      s_part.reshape(2, nm, CAP, half), w_edge, w_self, w_agg, w_node_out, u_mesh, slot_col, slope, latent)
    final = shape((width, width), F32)
    return pl.pallas_call(
        write_kernel,
        out_shape=(node, node, final, final, final),
        in_specs=[vmem()] * 6,
        out_specs=(vmem(),) * 5,
        compiler_params=params(),
        name="write",
    )(*outs)


def solution(mesh):
    split = P(("band", "mesh"), None)
    flat = P(("band", "mesh"))
    return jax.shard_map(
        functools.partial(shards, mesh.shape["band"], mesh.shape["mesh"]),
        mesh=mesh,
        in_specs=(split, split, split, flat, flat) + (P(),) * 12,
        out_specs=(split, split, P(), P(), P()),
        check_vma=False,
    )
```

```python
import functools

import jax
import jax.numpy as jnp
from jax import lax
from jax.experimental import pallas as pl
from jax.experimental.pallas import tpu as pltpu
from jax.sharding import PartitionSpec as P

CAP = 48
MESH = pl.DeviceIdType.MESH
F32 = jnp.float32
BF16 = jnp.bfloat16
MIB = 1024 * 1024


EB = 512
TB = 256


def sigmoid(v):
    return 0.5 + 0.5 * jnp.tanh(0.5 * v)


def dot(a, b):
    return jnp.dot(a, b, preferred_element_type=F32)


def dot_nt(a, b):
    return lax.dot_general(a, b, (((1,), (1,)), ((), ())), preferred_element_type=F32)


def dot_tn(a, b):
    return lax.dot_general(a, b, (((0,), (0,)), ((), ())), preferred_element_type=F32)


def iota(shape, dim):
    return lax.broadcasted_iota(jnp.int32, shape, dim)


def onehot(mask):
    return jnp.where(mask, 1.0, 0.0).astype(BF16)


def enter(axes):
    barrier = pltpu.get_barrier_semaphore()
    total = 0
    for axis, n in axes:
        me = lax.axis_index(axis)
        for d in range(1, n):
            pl.semaphore_signal(
                barrier, inc=1, device_id={axis: lax.rem(me + d, n)}, device_id_type=MESH
            )
        total += n - 1
    pl.semaphore_wait(barrier, total)


def send_all(axis, n, src, dst, send_sem, recv_sem):
    me = lax.axis_index(axis)
    copies = []
    for d in range(1, n):
        peer = lax.rem(me + d, n)
        copy = pltpu.make_async_remote_copy(
            src_ref=src(peer),
            dst_ref=dst(me),
            send_sem=send_sem.at[d],
            recv_sem=recv_sem.at[d],
            device_id={axis: peer},
            device_id_type=MESH,
        )
        copy.start()
        copies.append(copy)
    return copies


def wait_all(copies):
    for copy in copies:
        copy.wait()


def columns(rows_ref, out_ref):
    rows = rows_ref.shape[0]
    values = rows_ref[...].astype(F32)
    pad = jnp.zeros((128 - rows, 128), F32)
    turned = jnp.transpose(jnp.concatenate([values, pad], axis=0))
    for r in range(rows):
        out_ref[r * 128 : (r + 1) * 128, :] = jnp.broadcast_to(
            turned[:, r : r + 1], (128, 128)
        ).astype(jnp.int32)


def fetch_kernel(
    nb, nm, em, eg, gv, ml, w_in, b_in, w_out, gain, u_grid, u_mesh,
    table, rows_in, pick, latent_t, pre_grid, slots, slot_col, local_grid,
    grid_col, pgrid, left, right, ids_out, ids_in, asked, landed, padded, s1, r1, s2, r2,
):
    mesh_dev = ml.shape[0]
    grid_dev = gv.shape[1]
    rows = em.shape[0]
    me = lax.axis_index("mesh")
    band = lax.axis_index("band")
    enter((("mesh", nm),))
    x = em[...] - band * (nm * mesh_dev)
    lane = iota(x.shape, 1)
    row = iota(x.shape, 0)
    prev = pltpu.roll(x, 1, 1)
    prev = jnp.where(lane == 0, pltpu.roll(prev, 1, 0), prev)
    fresh = jnp.where((x != prev) | ((lane == 0) & (row == 0)), 1.0, 0.0)
    fb = fresh.astype(BF16)
    upper = onehot(iota((128, 128), 0) <= iota((128, 128), 1))
    totals = dot(fb, jnp.ones((128, 128), BF16)).astype(BF16)
    lower = onehot(iota((rows, rows), 1) < iota((rows, rows), 0))
    rank = dot(fb, upper) + dot(lower, totals) - 1.0
    owner = jnp.zeros(x.shape, jnp.int32)
    first = jnp.zeros(x.shape, F32)
    for o in range(1, nm):
        later = x >= o * mesh_dev
        begun = jnp.sum(jnp.where(later, 0.0, fresh), keepdims=True)
        owner = owner + jnp.where(later, 1, 0)
        first = jnp.where(later, begun, first)
    inner = (rank - first).astype(jnp.int32)
    slots[...] = owner * CAP + inner
    node = x - owner * mesh_dev
    high = jnp.right_shift(node, 4)
    low = node - high * 16
    high = jnp.where(fresh > 0, high, 0).astype(F32)
    low = jnp.where(fresh > 0, low, 0).astype(F32)
    owner_id = iota((nm, 128), 0)
    inner_id = iota((128, 128), 0)
    for r in range(rows):
        cut = slice(r * 128, (r + 1) * 128)
        mine = owner[r : r + 1, :] == owner_id
        left[0:nm, cut] = jnp.where(mine, high[r : r + 1, :], 0.0).astype(BF16)
        left[nm : 2 * nm, cut] = jnp.where(mine, low[r : r + 1, :], 0.0).astype(BF16)
        right[:, cut] = onehot(inner[r : r + 1, :] == inner_id)
    both = dot_nt(left[...], right[...])
    ids = both[0:nm] * 16.0 + both[nm : 2 * nm]
    for o in range(nm):
        ids_out[o] = jnp.broadcast_to(ids[o : o + 1, :], (8, 128))
    sent = send_all("mesh", nm, lambda p: ids_out.at[p], lambda q: ids_in.at[q], s1, r1)
    ids_in[me] = ids_out[me]
    padded[0:mesh_dev, :] = ml[...]
    padded[mesh_dev:, :] = jnp.zeros((padded.shape[0] - mesh_dev, padded.shape[1]), BF16)
    columns(slots, slot_col)
    local_grid[...] = eg[...] - (band * nm + me) * grid_dev
    columns(local_grid, grid_col)
    wait_all(sent)
    turned = jnp.transpose(ids_in[...].reshape(nm * 8, 128))
    for q in range(nm):
        ids_q = jnp.broadcast_to(turned[0:CAP, q * 8 : q * 8 + 1], (CAP, 128)).astype(jnp.int32)
        for t in range(pick.shape[1] // 128):
            pick[q * CAP : (q + 1) * CAP, t * 128 : (t + 1) * 128] = onehot(
                ids_q == iota((CAP, 128), 1) + t * 128
            )
    asked[...] = dot(pick[...], padded[...]).astype(BF16).reshape(asked.shape)
    sent = send_all("mesh", nm, lambda p: asked.at[p], lambda q: landed.at[q], s2, r2)
    landed[me] = asked[me]
    step = 256

    def grid_rows(i, carry):
        cut = pl.ds(pl.multiple_of(i * step, step), step)
        v = dot_tn(gv[:, cut], w_in[...]) + b_in[...]
        hidden = (v * sigmoid(v)).astype(BF16)
        y = dot(hidden, w_out[...])
        centred = y - jnp.mean(y, axis=-1, keepdims=True)
        var = jnp.mean(centred * centred, axis=-1, keepdims=True)
        lat = centred * lax.rsqrt(var + 1e-05) * gain[...]
        latent_t[:, cut] = jnp.transpose(lat).astype(BF16)
        pgrid[cut, :] = dot(lat.astype(BF16), u_grid[...]).astype(BF16)
        return carry

    lax.fori_loop(0, grid_dev // step, grid_rows, 0)

    def grid_edges(b, carry):
        cut = pl.ds(pl.multiple_of(b * EB, EB), EB)
        gcol = grid_col[cut, :]
        hot = jnp.concatenate(
            [onehot(gcol == iota((EB, 128), 1) + t * 128) for t in range(grid_dev // 128)], axis=1
        )
        pre_grid[cut, :] = dot(hot, pgrid[...]).astype(BF16)
        return carry

    lax.fori_loop(0, rows * 128 // EB, grid_edges, 0)
    wait_all(sent)
    rows_in[...] = landed[...].reshape(rows_in.shape)
    table[...] = dot(rows_in[...], u_mesh[...]).astype(BF16)


def edge_kernel(slot_s, slots, slot_col, table, pre_grid, b_edge, a_out, s_out, slope, acc, pre, both):
    rows = slots.shape[0]
    width = table.shape[1]
    tiles = table.shape[0] // TB
    per = EB // 128
    acc[...] = jnp.zeros_like(acc)

    def block(b, carry):
        cut = pl.ds(pl.multiple_of(b * EB, EB), EB)
        pre[...] = pre_grid[cut, :].astype(F32) + b_edge[...]
        low = slot_s[b * per, 0]
        high = slot_s[b * per + per - 1, 127]
        for t in range(tiles):
            @pl.when((low < (t + 1) * TB) & (high >= t * TB))
            def _():
                scol = slot_col[cut, :]
                hot = jnp.concatenate(
                    [onehot(scol == iota((EB, 128), 1) + (t * TB + u * 128)) for u in range(TB // 128)],
                    axis=1,
                )
                pre[...] += dot(hot, table[t * TB : (t + 1) * TB, :])

        v = pre[...]
        s = sigmoid(v)
        act = v * s
        both[:, 0:width] = act.astype(BF16)
        sl = (s + act * (1.0 - s)).astype(BF16)
        both[:, width:] = sl
        slope[cut, :] = sl
        for t in range(tiles):
            @pl.when((low < (t + 1) * TB) & (high >= t * TB))
            def _():
                hot = jnp.concatenate(
                    [onehot(slots[pl.ds(b * per + u, 1), :] == iota((TB, 128), 0) + t * TB) for u in range(per)],
                    axis=1,
                )
                acc[t * TB : (t + 1) * TB, :] += dot(hot, both[...])

        return carry

    lax.fori_loop(0, rows // per, block, 0)
    a_out[...] = acc[:, 0:width].astype(BF16)
    half = width // 2
    for c in range(2):
        s_out[c] = acc[:, width + c * half : width + (c + 1) * half].astype(BF16)


def make_sum(axes, scale, big, small, width, in1, mid, in2, all2, all1, q1, q2, q3, q4):
    n, m = axes[big], axes[small]
    rows = in1.shape[1]
    live = {}

    def add(ref, count):
        total = ref[0].astype(F32)
        for q in range(1, count):
            total = total + ref[q].astype(F32)
        return total

    def start(src):
        def part(p):
            return src.at[pl.ds(pl.multiple_of(p * rows, 16), rows), :]

        live[1] = send_all(big, n, part, lambda q: in1.at[q], q1.at[0], q1.at[1])
        me = lax.axis_index(big)
        in1[me] = src[pl.ds(pl.multiple_of(me * rows, 16), rows), :]

    def spread_big(values):
        me = lax.axis_index(big)
        all1[me] = values.astype(BF16)
        live[4] = send_all(big, n, lambda p: all1.at[me], lambda q: all1.at[q], q4.at[0], q4.at[1])

    def finish(out):
        wait_all(live[4])
        out[...] = all1[...].reshape(out.shape)

    if small == "band":

        def middle():
            wait_all(live[1])
            mid[...] = add(in1, n).astype(BF16)
            live[2] = send_all(small, m, lambda p: mid, lambda q: in2.at[q], q2.at[0], q2.at[1])
            in2[lax.axis_index(small)] = mid[...]

        def gather():
            wait_all(live[2])
            spread_big(add(in2, m) * scale)

        return start, middle, gather, None, finish

    pr, pc = mid.shape[1], mid.shape[2]
    cols = width // pc

    def middle():
        wait_all(live[1])
        total = add(in1, n)
        for i in range(m):
            a, c = i // cols, i % cols
            mid[i] = total[a * pr : (a + 1) * pr, c * pc : (c + 1) * pc]
        live[2] = send_all(small, m, lambda p: mid.at[p], lambda q: in2.at[q], q2.at[0], q2.at[1])
        me = lax.axis_index(small)
        in2[me] = mid[me]

    def gather():
        wait_all(live[2])
        me = lax.axis_index(small)
        all2[me] = add(in2, m) * scale
        live[3] = send_all(small, m, lambda p: all2.at[me], lambda q: all2.at[q], q3.at[0], q3.at[1])

    def spread():
        wait_all(live[3])
        spread_big(jnp.concatenate(
            [jnp.concatenate([all2[a * cols + c] for c in range(cols)], axis=1) for a in range(m // cols)],
            axis=0,
        ))

    return start, middle, gather, spread, finish


GB = 1024


def back_kernel(
    nb, nm, scale, pick, ml, ct, b_node, grid_rows, a_part, s_part, w_edge, w_self, w_agg,
    w_node, u_mesh, slot_col, slope, latent_t, rows_in,
    mesh_out, grad_mesh, oe, ou0, ou1, og0, og1,
    a_in, s_in, asked, landed, hot_s, lat_e, rows_t, acc, ge, gg, gu,
    sa, ra, ss, rs, sh, rh, *sums,
):
    mesh_dev, width = ml.shape
    half = width // 2
    rows = grid_rows.shape[0]
    slots_n = hot_s.shape[1]
    grid_dev = latent_t.shape[1]
    flat = nm * CAP
    me = lax.axis_index("mesh")
    axes = {"band": nb, "mesh": nm}
    sum_e, sum_u0, sum_u1, sum_g0, sum_g1 = [
        make_sum(axes, scale, big, small, w, *sums[i * 9 : (i + 1) * 9])
        for i, (big, small, w) in enumerate(
            (("band", "mesh", width),) + (("band", "mesh", half),) * 2 + (("mesh", "band", half),) * 2
        )
    ]
    sum_u, sum_g = (sum_u0, sum_u1), (sum_g0, sum_g1)

    def send_slopes(c):
        s_in[c, me] = s_part[c, me]
        return send_all("mesh", nm, lambda p: s_part.at[c, p], lambda q: s_in.at[c, q], ss.at[c], rs.at[c])

    enter((("mesh", nm), ("band", nb)))
    sent_a = send_all("mesh", nm, lambda p: a_part.at[p], lambda q: a_in.at[q], sa, ra)
    sent_s = [send_slopes(0)]
    a_in[me] = a_part[me]
    own = dot(ml[...], w_self[...]) + b_node[...]
    back = dot_nt(ct[...], w_node[...])

    def build(b, carry):
        cut = pl.ds(pl.multiple_of(b * EB, EB), EB)
        per = EB // 128
        hot = jnp.concatenate(
            [onehot(grid_rows[pl.ds(b * per + u, 1), :] == iota((grid_dev, 128), 0)) for u in range(per)],
            axis=1,
        )
        lat_e[:, cut] = dot(latent_t[...], hot).astype(BF16)
        scol = slot_col[cut, :]
        for t in range(slots_n // 128):
            hot_s[cut, t * 128 : (t + 1) * 128] = onehot(scol == iota((EB, 128), 1) + t * 128)
        return carry

    lax.fori_loop(0, rows * 128 // EB, build, 0)
    rows_t[...] = jnp.transpose(rows_in[...].astype(F32)).astype(BF16)
    wait_all(sent_a)
    acts = dot_tn(pick[...], a_in[...].reshape(flat, width))[0:mesh_dev].astype(BF16)
    agg = dot(acts, w_edge[...]).astype(BF16)
    node_pre = own + dot(agg, w_agg[...])
    s = sigmoid(node_pre)
    node_act = node_pre * s
    g_node = (back * (s + node_act * (1.0 - s))).astype(BF16)
    g_agg = dot_nt(g_node, w_agg[...]).astype(BF16)
    h = dot_nt(g_agg, w_edge[...])
    hb = jnp.concatenate(
        [h.astype(BF16), jnp.zeros((pick.shape[1] - mesh_dev, width), BF16)], axis=0
    )
    sent_h = []
    for c in range(2):
        asked[c] = dot(pick[...], hb[:, c * half : (c + 1) * half]).astype(BF16).reshape(nm, CAP, half)
        sent_h.append(send_all("mesh", nm, lambda p, c=c: asked.at[c, p], lambda q, c=c: landed.at[c, q],
                               sh.at[c], rh.at[c]))
        landed[c, me] = asked[c, me]
    ge[...] = dot_tn(acts, g_agg).astype(BF16)
    sum_e[0](ge)
    mesh_out[...] = (ml[...].astype(F32) + dot(node_act.astype(BF16), w_node[...])).astype(BF16)
    part = ct[...].astype(F32) + dot_nt(g_node, w_self[...])

    def halves(c):
        acc[...] = jnp.zeros_like(acc)
        col = slice(c * half, (c + 1) * half)

        def block(b, carry):
            cut = pl.ds(pl.multiple_of(b * GB, GB), GB)
            g = (dot(hot_s[cut, :], table) * slope[cut, col].astype(F32)).astype(BF16)
            acc[...] += dot(lat_e[:, cut], g)
            return carry

        wait_all(sent_h[c])
        table = landed[c].reshape(flat, half)
        lax.fori_loop(0, rows * 128 // GB, block, 0)
        gg[c] = acc[...].astype(BF16)
        sum_g[c][0](gg.at[c])
        pm = (table.astype(F32) * s_part[c].reshape(flat, half).astype(F32)).astype(BF16)
        gu[c] = dot(rows_t[...], pm).astype(BF16)
        sum_u[c][0](gu.at[c])

    halves(0)
    sum_e[1]()
    halves(1)
    sent_s.append(send_slopes(1))
    sum_g0[1]()
    sum_u0[1]()
    sum_e[2]()
    sum_g1[1]()
    sum_u1[1]()
    sum_g0[2]()
    sum_u0[2]()
    sum_e[3]()
    sum_g1[2]()
    sum_u1[2]()
    sum_u0[3]()
    wait_all(sent_s[0])
    wait_all(sent_s[1])
    slopes = jnp.concatenate(
        [dot_tn(pick[...], s_in[c].reshape(flat, half))[0:mesh_dev] for c in range(2)], axis=1
    )
    g_pmesh = (h * slopes).astype(BF16)
    sum_u1[3]()
    grad_mesh[...] = (part + dot_nt(g_pmesh, u_mesh[...])).astype(BF16)
    sum_e[4](oe)
    sum_g0[4](og0)
    sum_u0[4](ou0)
    sum_g1[4](og1)
    sum_u1[4](ou1)


def write_kernel(mo, gm, e, u0, u1, g0, g1, mo_out, gm_out, e_out, g_out, u_out):
    half = g0.shape[1]
    mo_out[...] = mo[...]
    gm_out[...] = gm[...]
    e_out[...] = e[...].astype(F32)
    u_out[:, 0:half] = u0[...].astype(F32)
    u_out[:, half:] = u1[...].astype(F32)
    g_out[:, 0:half] = g0[...].astype(F32)
    g_out[:, half:] = g1[...].astype(F32)


def vmem():
    return pl.BlockSpec(memory_space=pltpu.VMEM)


def shape(dims, kind):
    return jax.ShapeDtypeStruct(dims, kind)


def params(mib, cid=None):
    if cid is None:
        return pltpu.CompilerParams(vmem_limit_bytes=mib * MIB)
    return pltpu.CompilerParams(
        vmem_limit_bytes=mib * MIB, collective_id=cid, has_side_effects=True
    )


def shards(
    nb, nm, grid_vars, mesh_latent, cotangent, edge_grid, edge_mesh, w_in, b_in, w_out, norm_gain,
    u_grid, u_mesh, b_edge, w_edge, w_self, w_agg, b_node, w_node_out,
):
    grid_dev = grid_vars.shape[0]
    mesh_dev, width = mesh_latent.shape
    edges = edge_grid.shape[0]
    rows = edges // 128
    slots_n = nm * CAP
    padded = -(-mesh_dev // 128) * 128
    sem = pltpu.SemaphoreType.DMA
    em = edge_mesh.reshape(rows, 128)
    eg = edge_grid.reshape(rows, 128)
    table, rows_in, pick, latent_t, pre_grid, slots, slot_col, local_grid = pl.pallas_call(
        functools.partial(fetch_kernel, nb, nm),
        out_shape=(
            shape((slots_n, width), BF16), shape((slots_n, width), BF16), shape((slots_n, padded), BF16),
            shape((width, grid_dev), BF16), shape((edges, width), BF16),
            shape((rows, 128), jnp.int32), shape((edges, 128), jnp.int32), shape((rows, 128), jnp.int32),
        ),
        in_specs=[vmem()] * 10,
        out_specs=(vmem(),) * 8,
        scratch_shapes=[
            pltpu.VMEM((edges, 128), jnp.int32), pltpu.VMEM((grid_dev, width), BF16),
            pltpu.VMEM((2 * nm, edges), BF16), pltpu.VMEM((128, edges), BF16),
            pltpu.VMEM((nm, 8, 128), F32), pltpu.VMEM((nm, 8, 128), F32),
            pltpu.VMEM((nm, CAP, width), BF16), pltpu.VMEM((nm, CAP, width), BF16),
            pltpu.VMEM((padded, width), BF16),
            sem((nm,)), sem((nm,)), sem((nm,)), sem((nm,)),
        ],
        compiler_params=params(20, 0),
        name="fetch",
    )(em, eg, grid_vars.T, mesh_latent, w_in, b_in.reshape(1, -1), w_out, norm_gain.reshape(1, -1),
      u_grid, u_mesh)
    half = width // 2
    a_part, s_part, slope = pl.pallas_call(
        edge_kernel,
        out_shape=(
            shape((slots_n, width), BF16), shape((2, slots_n, half), BF16), shape((edges, width), BF16),
        ),
        in_specs=[pl.BlockSpec(memory_space=pltpu.SMEM)] + [vmem()] * 5,
        out_specs=(vmem(),) * 3,
        scratch_shapes=[
            pltpu.VMEM((slots_n, 2 * width), F32), pltpu.VMEM((EB, width), F32),
            pltpu.VMEM((EB, 2 * width), BF16),
        ],
        compiler_params=params(16),
        name="edges",
    )(slots, slots, slot_col, table, pre_grid, b_edge.reshape(1, -1))
    sums = []
    for n, m, w in ((nb, nm, width), (nb, nm, half), (nb, nm, half), (nm, nb, half), (nm, nb, half)):
        big = width // n
        if n == nm:
            mid = [pltpu.VMEM((big, w), BF16), pltpu.VMEM((m, big, w), BF16), pltpu.VMEM((8, 128), F32)]
        else:
            across = min(m, w // 128)
            piece = pltpu.VMEM((m, big // (m // across), w // across), F32)
            mid = [piece] * 3
        sums += [pltpu.VMEM((n, big, w), BF16)] + mid + [
            pltpu.VMEM((n, big, w), BF16), sem((2, n)), sem((2, m)), sem((2, m)), sem((2, n)),
        ]
    scale = (edges * nb * nm) ** (-0.5)
    node = shape((mesh_dev, width), BF16)
    slim = shape((width, half), BF16)
    blocks = pltpu.VMEM((2, nm, CAP, half), BF16)
    outs = pl.pallas_call(
        functools.partial(back_kernel, nb, nm, scale),
        out_shape=(node, node, shape((width, width), BF16), slim, slim, slim, slim),
        in_specs=[vmem()] * 16,
        out_specs=(vmem(),) * 7,
        scratch_shapes=[
            pltpu.VMEM((nm, CAP, width), BF16), blocks, blocks, blocks,
            pltpu.VMEM((edges, slots_n), BF16), pltpu.VMEM((width, edges), BF16),
            pltpu.VMEM((width, slots_n), BF16), pltpu.VMEM((width, half), F32),
            pltpu.VMEM((width, width), BF16), pltpu.VMEM((2, width, half), BF16),
            pltpu.VMEM((2, width, half), BF16),
            sem((nm,)), sem((nm,)), sem((2, nm)), sem((2, nm)), sem((2, nm)), sem((2, nm)),
        ] + sums,
        compiler_params=params(38, 1),
        name="back",
    )(pick, mesh_latent, cotangent, b_node.reshape(1, -1), local_grid, a_part.reshape(nm, CAP, width),
      s_part.reshape(2, nm, CAP, half), w_edge, w_self, w_agg, w_node_out, u_mesh, slot_col, slope, latent_t,
      rows_in)
    final = shape((width, width), F32)
    return pl.pallas_call(
        write_kernel,
        out_shape=(node, node, final, final, final),
        in_specs=[vmem()] * 7,
        out_specs=(vmem(),) * 5,
        compiler_params=params(16),
        name="write",
    )(*outs)


def solution(mesh):
    split = P(("band", "mesh"), None)
    flat = P(("band", "mesh"))
    return jax.shard_map(
        functools.partial(shards, mesh.shape["band"], mesh.shape["mesh"]),
        mesh=mesh,
        in_specs=(split, split, split, flat, flat) + (P(),) * 12,
        out_specs=(split, split, P(), P(), P()),
        check_vma=False,
    )
```

```python
import functools

import jax
import jax.numpy as jnp
from jax import lax
from jax.experimental import pallas as pl
from jax.experimental.pallas import tpu as pltpu
from jax.sharding import PartitionSpec as P

CAP = 48
MESH = pl.DeviceIdType.MESH
F32 = jnp.float32
BF16 = jnp.bfloat16
MIB = 1024 * 1024


EB = 512
TB = 256


def sigmoid(v):
    return 0.5 + 0.5 * jnp.tanh(0.5 * v)


def dot(a, b):
    return jnp.dot(a, b, preferred_element_type=F32)


def dot_nt(a, b):
    return lax.dot_general(a, b, (((1,), (1,)), ((), ())), preferred_element_type=F32)


def dot_tn(a, b):
    return lax.dot_general(a, b, (((0,), (0,)), ((), ())), preferred_element_type=F32)


def iota(shape, dim):
    return lax.broadcasted_iota(jnp.int32, shape, dim)


def onehot(mask):
    return jnp.where(mask, 1.0, 0.0).astype(BF16)


def greet(axes):
    barrier = pltpu.get_barrier_semaphore()
    for axis, n in axes:
        me = lax.axis_index(axis)
        for d in range(1, n):
            pl.semaphore_signal(
                barrier, inc=1, device_id={axis: lax.rem(me + d, n)}, device_id_type=MESH
            )


def gathered(axes):
    pl.semaphore_wait(pltpu.get_barrier_semaphore(), sum(n - 1 for _, n in axes))


def send_all(axis, n, src, dst, send_sem, recv_sem):
    me = lax.axis_index(axis)
    copies = []
    for d in range(1, n):
        peer = lax.rem(me + d, n)
        copy = pltpu.make_async_remote_copy(
            src_ref=src(peer),
            dst_ref=dst(me),
            send_sem=send_sem.at[d],
            recv_sem=recv_sem.at[d],
            device_id={axis: peer},
            device_id_type=MESH,
        )
        copy.start()
        copies.append(copy)
    return copies


def wait_all(copies):
    for copy in copies:
        copy.wait()


def columns(rows_ref, out_ref):
    rows = rows_ref.shape[0]
    values = rows_ref[...].astype(F32)
    pad = jnp.zeros((128 - rows, 128), F32)
    turned = jnp.transpose(jnp.concatenate([values, pad], axis=0))
    for r in range(rows):
        out_ref[r * 128 : (r + 1) * 128, :] = jnp.broadcast_to(
            turned[:, r : r + 1], (128, 128)
        ).astype(jnp.int32)


def fetch_kernel(
    nb, nm, em_h, eg_h, gv_h, ml_h, w_in_h, b_in_h, w_out_h, gain_h, u_grid_h, u_mesh_h, b_edge_h,
    table, rows_in, pick, latent_t, pre_grid, slots, slot_col, local_grid, b_edge,
    em, eg, gv, ml, w_in, b_in, w_out, gain, u_grid, u_mesh, load_sem, grid_col, pgrid, left, right, ids_out, ids_in, asked, landed, padded, s1, r1, s2, r2,
):
    mesh_dev = ml.shape[0]
    grid_dev = gv.shape[1]
    rows = em.shape[0]
    me = lax.axis_index("mesh")
    band = lax.axis_index("band")
    loads = []
    for i, (src, dst) in enumerate(
        ((em_h, em), (eg_h, eg), (ml_h, ml), (gv_h, gv), (w_in_h, w_in), (b_in_h, b_in), (w_out_h, w_out),
         (gain_h, gain), (u_grid_h, u_grid), (u_mesh_h, u_mesh), (b_edge_h, b_edge))
    ):
        copy = pltpu.make_async_copy(src, dst, load_sem.at[i])
        copy.start()
        loads.append(copy)
    everyone = (("mesh", nm),)
    greet(everyone)
    loads[0].wait()
    x = em[...] - band * (nm * mesh_dev)
    lane = iota(x.shape, 1)
    row = iota(x.shape, 0)
    prev = pltpu.roll(x, 1, 1)
    prev = jnp.where(lane == 0, pltpu.roll(prev, 1, 0), prev)
    fresh = jnp.where((x != prev) | ((lane == 0) & (row == 0)), 1.0, 0.0)
    fb = fresh.astype(BF16)
    upper = onehot(iota((128, 128), 0) <= iota((128, 128), 1))
    totals = dot(fb, jnp.ones((128, 128), BF16)).astype(BF16)
    lower = onehot(iota((rows, rows), 1) < iota((rows, rows), 0))
    rank = dot(fb, upper) + dot(lower, totals) - 1.0
    owner = jnp.zeros(x.shape, jnp.int32)
    first = jnp.zeros(x.shape, F32)
    for o in range(1, nm):
        later = x >= o * mesh_dev
        begun = jnp.sum(jnp.where(later, 0.0, fresh), keepdims=True)
        owner = owner + jnp.where(later, 1, 0)
        first = jnp.where(later, begun, first)
    inner = (rank - first).astype(jnp.int32)
    slots[...] = owner * CAP + inner
    node = x - owner * mesh_dev
    high = jnp.right_shift(node, 4)
    low = node - high * 16
    high = jnp.where(fresh > 0, high, 0).astype(F32)
    low = jnp.where(fresh > 0, low, 0).astype(F32)
    owner_id = iota((nm, 128), 0)
    inner_id = iota((128, 128), 0)
    for r in range(rows):
        cut = slice(r * 128, (r + 1) * 128)
        mine = owner[r : r + 1, :] == owner_id
        left[0:nm, cut] = jnp.where(mine, high[r : r + 1, :], 0.0).astype(BF16)
        left[nm : 2 * nm, cut] = jnp.where(mine, low[r : r + 1, :], 0.0).astype(BF16)
        right[:, cut] = onehot(inner[r : r + 1, :] == inner_id)
    both = dot_nt(left[...], right[...])
    ids = both[0:nm] * 16.0 + both[nm : 2 * nm]
    for o in range(nm):
        ids_out[o] = jnp.broadcast_to(ids[o : o + 1, :], (8, 128))
    gathered(everyone)
    sent = send_all("mesh", nm, lambda p: ids_out.at[p], lambda q: ids_in.at[q], s1, r1)
    ids_in[me] = ids_out[me]
    for copy in loads[1:3]:
        copy.wait()
    padded[0:mesh_dev, :] = ml[...]
    padded[mesh_dev:, :] = jnp.zeros((padded.shape[0] - mesh_dev, padded.shape[1]), BF16)
    columns(slots, slot_col)
    local_grid[...] = eg[...] - (band * nm + me) * grid_dev
    columns(local_grid, grid_col)
    wait_all(sent)
    turned = jnp.transpose(ids_in[...].reshape(nm * 8, 128))
    for q in range(nm):
        ids_q = jnp.broadcast_to(turned[0:CAP, q * 8 : q * 8 + 1], (CAP, 128)).astype(jnp.int32)
        for t in range(pick.shape[1] // 128):
            pick[q * CAP : (q + 1) * CAP, t * 128 : (t + 1) * 128] = onehot(
                ids_q == iota((CAP, 128), 1) + t * 128
            )
    asked[...] = dot(pick[...], padded[...]).astype(BF16).reshape(asked.shape)
    sent = send_all("mesh", nm, lambda p: asked.at[p], lambda q: landed.at[q], s2, r2)
    landed[me] = asked[me]
    for copy in loads[3:]:
        copy.wait()
    step = 256

    def grid_rows(i, carry):
        cut = pl.ds(pl.multiple_of(i * step, step), step)
        v = dot_tn(gv[:, cut], w_in[...]) + b_in[...]
        hidden = (v * sigmoid(v)).astype(BF16)
        y = dot(hidden, w_out[...])
        centred = y - jnp.mean(y, axis=-1, keepdims=True)
        var = jnp.mean(centred * centred, axis=-1, keepdims=True)
        lat = centred * lax.rsqrt(var + 1e-05) * gain[...]
        latent_t[:, cut] = jnp.transpose(lat).astype(BF16)
        pgrid[cut, :] = dot(lat.astype(BF16), u_grid[...]).astype(BF16)
        return carry

    lax.fori_loop(0, grid_dev // step, grid_rows, 0)

    def grid_edges(b, carry):
        cut = pl.ds(pl.multiple_of(b * EB, EB), EB)
        gcol = grid_col[cut, :]
        hot = jnp.concatenate(
            [onehot(gcol == iota((EB, 128), 1) + t * 128) for t in range(grid_dev // 128)], axis=1
        )
        pre_grid[cut, :] = dot(hot, pgrid[...]).astype(BF16)
        return carry

    lax.fori_loop(0, rows * 128 // EB, grid_edges, 0)
    wait_all(sent)
    rows_in[...] = landed[...].reshape(rows_in.shape)
    table[...] = dot(rows_in[...], u_mesh[...]).astype(BF16)


def edge_kernel(slot_s, slots, slot_col, table, pre_grid, b_edge, a_out, s_out, slope, acc, pre, both):
    rows = slots.shape[0]
    width = table.shape[1]
    tiles = table.shape[0] // TB
    per = EB // 128
    acc[...] = jnp.zeros_like(acc)

    def finish(v):
        s = sigmoid(v)
        act = v * s
        return act.astype(BF16), (s + act * (1.0 - s)).astype(BF16)

    def block(b, carry):
        cut = pl.ds(pl.multiple_of(b * EB, EB), EB)
        low = slot_s[b * per, 0]
        high = slot_s[b * per + per - 1, 127]
        base = pl.multiple_of(jnp.right_shift(low, TB.bit_length() - 1) * TB, TB)
        single = high < base + TB

        @pl.when(single)
        def _():
            window = table[pl.ds(base, TB), :]
            for u in range(per):
                part = pl.ds(pl.multiple_of(b * EB + u * 128, 128), 128)
                scol = slot_col[part, :] - base
                hot = jnp.concatenate([onehot(scol == iota((128, 128), 1) + w * 128) for w in range(TB // 128)], axis=1)
                v = pre_grid[part, :].astype(F32) + b_edge[...] + dot(hot, window)
                act, sl = finish(v)
                both[u * 128 : (u + 1) * 128, 0:width] = act
                both[u * 128 : (u + 1) * 128, width:] = sl
                slope[part, :] = sl
            hot = jnp.concatenate(
                [onehot(slots[pl.ds(b * per + u, 1), :] - base == iota((TB, 128), 0)) for u in range(per)],
                axis=1,
            )
            acc[pl.ds(base, TB), :] += dot(hot, both[...])

        @pl.when(jnp.logical_not(single))
        def _():
            pre[...] = pre_grid[cut, :].astype(F32) + b_edge[...]
            for t in range(tiles):
                @pl.when((low < (t + 1) * TB) & (high >= t * TB))
                def _():
                    scol = slot_col[cut, :]
                    hot = jnp.concatenate(
                        [onehot(scol == iota((EB, 128), 1) + (t * TB + u * 128)) for u in range(TB // 128)],
                        axis=1,
                    )
                    pre[...] += dot(hot, table[t * TB : (t + 1) * TB, :])

            act, sl = finish(pre[...])
            both[:, 0:width] = act
            both[:, width:] = sl
            slope[cut, :] = sl
            for t in range(tiles):
                @pl.when((low < (t + 1) * TB) & (high >= t * TB))
                def _():
                    hot = jnp.concatenate(
                        [onehot(slots[pl.ds(b * per + u, 1), :] == iota((TB, 128), 0) + t * TB) for u in range(per)],
                        axis=1,
                    )
                    acc[t * TB : (t + 1) * TB, :] += dot(hot, both[...])

        return carry

    lax.fori_loop(0, rows // per, block, 0)
    a_out[...] = acc[:, 0:width].astype(BF16)
    half = width // 2
    for c in range(2):
        s_out[c] = acc[:, width + c * half : width + (c + 1) * half].astype(BF16)


def make_sum(axes, scale, big, small, width, all1, in1, mid, in2, all2, q1, q2, q3, q4):
    n, m = axes[big], axes[small]
    rows = in1.shape[1]
    live = {}

    def add(ref, count):
        total = ref[0].astype(F32)
        for q in range(1, count):
            total = total + ref[q].astype(F32)
        return total

    def start(src):
        def part(p):
            return src.at[pl.ds(pl.multiple_of(p * rows, 16), rows), :]

        live[1] = send_all(big, n, part, lambda q: in1.at[q], q1.at[0], q1.at[1])
        me = lax.axis_index(big)
        in1[me] = src[pl.ds(pl.multiple_of(me * rows, 16), rows), :]

    def spread_big(values):
        me = lax.axis_index(big)
        all1[me] = values.astype(BF16)
        live[4] = send_all(big, n, lambda p: all1.at[me], lambda q: all1.at[q], q4.at[0], q4.at[1])

    def finish():
        wait_all(live[4])

    if small == "band":

        def middle():
            wait_all(live[1])
            mid[...] = add(in1, n).astype(BF16)
            live[2] = send_all(small, m, lambda p: mid, lambda q: in2.at[q], q2.at[0], q2.at[1])
            in2[lax.axis_index(small)] = mid[...]

        def gather():
            wait_all(live[2])
            spread_big(add(in2, m) * scale)

        return start, middle, gather, None, finish

    pr, pc = mid.shape[1], mid.shape[2]
    cols = width // pc

    def middle():
        wait_all(live[1])
        total = add(in1, n)
        for i in range(m):
            a, c = i // cols, i % cols
            mid[i] = total[a * pr : (a + 1) * pr, c * pc : (c + 1) * pc]
        live[2] = send_all(small, m, lambda p: mid.at[p], lambda q: in2.at[q], q2.at[0], q2.at[1])
        me = lax.axis_index(small)
        in2[me] = mid[me]

    def gather():
        wait_all(live[2])
        me = lax.axis_index(small)
        all2[me] = add(in2, m) * scale
        live[3] = send_all(small, m, lambda p: all2.at[me], lambda q: all2.at[q], q3.at[0], q3.at[1])

    def spread():
        wait_all(live[3])
        spread_big(jnp.concatenate(
            [jnp.concatenate([all2[a * cols + c] for c in range(cols)], axis=1) for a in range(m // cols)],
            axis=0,
        ))

    return start, middle, gather, spread, finish


GB = 1024


def back_kernel(
    nb, nm, scale, pick, ml, ct, b_node, grid_rows, a_part, s_part, w_edge, w_self, w_agg,
    w_node, u_mesh, slot_col, slope, latent_t, rows_in,
    mesh_out, grad_mesh, oe, ou0, ou1, og0, og1,
    a_in, s_in, asked, landed, hot_s, lat_e, rows_t, acc, ge, gg, gu,
    sa, ra, ss, rs, sh, rh, *sums,
):
    mesh_dev, width = ml.shape
    half = width // 2
    rows = grid_rows.shape[0]
    slots_n = hot_s.shape[1]
    grid_dev = latent_t.shape[1]
    flat = nm * CAP
    me = lax.axis_index("mesh")
    axes = {"band": nb, "mesh": nm}
    sum_e, sum_u0, sum_u1, sum_g0, sum_g1 = [
        make_sum(axes, scale, big, small, w, (oe, ou0, ou1, og0, og1)[i], *sums[i * 8 : (i + 1) * 8])
        for i, (big, small, w) in enumerate(
            (("band", "mesh", width),) + (("band", "mesh", half),) * 2 + (("mesh", "band", half),) * 2
        )
    ]
    sum_u, sum_g = (sum_u0, sum_u1), (sum_g0, sum_g1)

    def send_slopes(c):
        s_in[c, me] = s_part[c, me]
        return send_all("mesh", nm, lambda p: s_part.at[c, p], lambda q: s_in.at[c, q], ss.at[c], rs.at[c])

    everyone = (("mesh", nm), ("band", nb))
    greet(everyone)
    gathered(everyone)
    sent_a = send_all("mesh", nm, lambda p: a_part.at[p], lambda q: a_in.at[q], sa, ra)
    sent_s = [send_slopes(0)]
    a_in[me] = a_part[me]
    own = dot(ml[...], w_self[...]) + b_node[...]
    back = dot_nt(ct[...], w_node[...])

    def build(b, carry):
        cut = pl.ds(pl.multiple_of(b * EB, EB), EB)
        per = EB // 128
        hot = jnp.concatenate(
            [onehot(grid_rows[pl.ds(b * per + u, 1), :] == iota((grid_dev, 128), 0)) for u in range(per)],
            axis=1,
        )
        lat_e[:, cut] = dot(latent_t[...], hot).astype(BF16)
        scol = slot_col[cut, :]
        for t in range(slots_n // 128):
            hot_s[cut, t * 128 : (t + 1) * 128] = onehot(scol == iota((EB, 128), 1) + t * 128)
        return carry

    lax.fori_loop(0, rows * 128 // EB, build, 0)
    rows_t[...] = jnp.transpose(rows_in[...].astype(F32)).astype(BF16)
    wait_all(sent_a)
    acts = dot_tn(pick[...], a_in[...].reshape(flat, width))[0:mesh_dev].astype(BF16)
    agg = dot(acts, w_edge[...]).astype(BF16)
    node_pre = own + dot(agg, w_agg[...])
    s = sigmoid(node_pre)
    node_act = node_pre * s
    g_node = (back * (s + node_act * (1.0 - s))).astype(BF16)
    g_agg = dot_nt(g_node, w_agg[...]).astype(BF16)
    h = dot_nt(g_agg, w_edge[...])
    hb = jnp.concatenate(
        [h.astype(BF16), jnp.zeros((pick.shape[1] - mesh_dev, width), BF16)], axis=0
    )
    sent_h = []
    for c in range(2):
        asked[c] = dot(pick[...], hb[:, c * half : (c + 1) * half]).astype(BF16).reshape(nm, CAP, half)
        sent_h.append(send_all("mesh", nm, lambda p, c=c: asked.at[c, p], lambda q, c=c: landed.at[c, q],
                               sh.at[c], rh.at[c]))
        landed[c, me] = asked[c, me]
    sent_s.append(send_slopes(1))
    ge[...] = dot_tn(acts, g_agg).astype(BF16)
    sum_e[0](ge)
    mesh_out[...] = (ml[...].astype(F32) + dot(node_act.astype(BF16), w_node[...])).astype(BF16)
    part = ct[...].astype(F32) + dot_nt(g_node, w_self[...])

    def halves(c, between):
        acc[...] = jnp.zeros_like(acc)
        col = slice(c * half, (c + 1) * half)
        wait_all(sent_h[c])
        table = landed[c].reshape(flat, half)
        pm = (table.astype(F32) * s_part[c].reshape(flat, half).astype(F32)).astype(BF16)
        gu[c] = dot(rows_t[...], pm).astype(BF16)
        sum_u[c][0](gu.at[c])
        for b in range(rows * 128 // GB):
            cut = slice(b * GB, (b + 1) * GB)
            g = (dot(hot_s[cut, :], table) * slope[cut, col].astype(F32)).astype(BF16)
            acc[...] += dot(lat_e[:, cut], g)
            if b in between:
                between[b]()
        gg[c] = acc[...].astype(BF16)
        sum_g[c][0](gg.at[c])

    last = rows * 128 // GB - 1
    halves(0, {min(1, last): sum_e[1]})
    halves(1, {0: sum_u0[1]})
    sum_e[2]()
    sum_u1[1]()
    sum_u0[2]()
    sum_g0[1]()
    wait_all(sent_s[0])
    wait_all(sent_s[1])
    slopes = jnp.concatenate(
        [dot_tn(pick[...], s_in[c].reshape(flat, half))[0:mesh_dev] for c in range(2)], axis=1
    )
    g_pmesh = (h * slopes).astype(BF16)
    grad_mesh[...] = (part + dot_nt(g_pmesh, u_mesh[...])).astype(BF16)
    sum_e[3]()
    sum_g0[2]()
    sum_u0[3]()
    sum_g1[1]()
    sum_u1[2]()
    sum_g1[2]()
    sum_u1[3]()
    sum_e[4]()
    sum_g0[4]()
    sum_u0[4]()
    sum_u1[4]()
    sum_g1[4]()


def write_kernel(mo, gm, e, u0, u1, g0, g1, mo_out, gm_out, e_out, g_out, u_out):
    half = g0.shape[1]
    mo_out[...] = mo[...]
    gm_out[...] = gm[...]
    e_out[...] = e[...].astype(F32)
    u_out[:, 0:half] = u0[...].astype(F32)
    u_out[:, half:] = u1[...].astype(F32)
    g_out[:, 0:half] = g0[...].astype(F32)
    g_out[:, half:] = g1[...].astype(F32)


def vmem():
    return pl.BlockSpec(memory_space=pltpu.VMEM)


def shape(dims, kind):
    return jax.ShapeDtypeStruct(dims, kind)


def params(mib, cid=None):
    if cid is None:
        return pltpu.CompilerParams(vmem_limit_bytes=mib * MIB)
    return pltpu.CompilerParams(
        vmem_limit_bytes=mib * MIB, collective_id=cid, has_side_effects=True
    )


def shards(
    nb, nm, grid_vars, mesh_latent, cotangent, edge_grid, edge_mesh, w_in, b_in, w_out, norm_gain,
    u_grid, u_mesh, b_edge, w_edge, w_self, w_agg, b_node, w_node_out,
):
    grid_dev = grid_vars.shape[0]
    mesh_dev, width = mesh_latent.shape
    edges = edge_grid.shape[0]
    rows = edges // 128
    slots_n = nm * CAP
    padded = -(-mesh_dev // 128) * 128
    sem = pltpu.SemaphoreType.DMA
    em = edge_mesh.reshape(rows, 128)
    eg = edge_grid.reshape(rows, 128)
    table, rows_in, pick, latent_t, pre_grid, slots, slot_col, local_grid, bias = pl.pallas_call(
        functools.partial(fetch_kernel, nb, nm),
        out_shape=(
            shape((slots_n, width), BF16), shape((slots_n, width), BF16), shape((slots_n, padded), BF16),
            shape((width, grid_dev), BF16), shape((edges, width), BF16),
            shape((rows, 128), jnp.int32), shape((edges, 128), jnp.int32), shape((rows, 128), jnp.int32),
            shape((1, width), F32),
        ),
        in_specs=[pl.BlockSpec(memory_space=pltpu.HBM)] * 11,
        out_specs=(vmem(),) * 9,
        scratch_shapes=[
            pltpu.VMEM((rows, 128), jnp.int32), pltpu.VMEM((rows, 128), jnp.int32),
            pltpu.VMEM((grid_vars.shape[1], grid_dev), BF16), pltpu.VMEM((mesh_dev, width), BF16),
            pltpu.VMEM((grid_vars.shape[1], width), BF16), pltpu.VMEM((1, width), F32),
            pltpu.VMEM((width, width), BF16), pltpu.VMEM((1, width), F32),
            pltpu.VMEM((width, width), BF16), pltpu.VMEM((width, width), BF16), sem((11,)),
            pltpu.VMEM((edges, 128), jnp.int32), pltpu.VMEM((grid_dev, width), BF16),
            pltpu.VMEM((2 * nm, edges), BF16), pltpu.VMEM((128, edges), BF16),
            pltpu.VMEM((nm, 8, 128), F32), pltpu.VMEM((nm, 8, 128), F32),
            pltpu.VMEM((nm, CAP, width), BF16), pltpu.VMEM((nm, CAP, width), BF16),
            pltpu.VMEM((padded, width), BF16),
            sem((nm,)), sem((nm,)), sem((nm,)), sem((nm,)),
        ],
        compiler_params=params(24, 0),
        name="fetch",
    )(*[
        pltpu.with_memory_space_constraint(v, pltpu.HBM)
        for v in (em, eg, grid_vars.T, mesh_latent, w_in, b_in.reshape(1, -1), w_out,
                  norm_gain.reshape(1, -1), u_grid, u_mesh, b_edge.reshape(1, -1))
    ])
    half = width // 2
    a_part, s_part, slope = pl.pallas_call(
        edge_kernel,
        out_shape=(
            shape((slots_n, width), BF16), shape((2, slots_n, half), BF16), shape((edges, width), BF16),
        ),
        in_specs=[pl.BlockSpec(memory_space=pltpu.SMEM)] + [vmem()] * 5,
        out_specs=(vmem(),) * 3,
        scratch_shapes=[
            pltpu.VMEM((slots_n, 2 * width), F32), pltpu.VMEM((EB, width), F32),
            pltpu.VMEM((EB, 2 * width), BF16),
        ],
        compiler_params=params(16),
        name="edges",
    )(slots, slots, slot_col, table, pre_grid, bias)
    sums = []
    for n, m, w in ((nb, nm, width), (nb, nm, half), (nb, nm, half), (nm, nb, half), (nm, nb, half)):
        big = width // n
        if n == nm:
            mid = [pltpu.VMEM((big, w), BF16), pltpu.VMEM((m, big, w), BF16), pltpu.VMEM((8, 128), F32)]
        else:
            across = min(m, w // 128)
            piece = pltpu.VMEM((m, big // (m // across), w // across), F32)
            mid = [piece] * 3
        sums += [pltpu.VMEM((n, big, w), BF16)] + mid + [
            sem((2, n)), sem((2, m)), sem((2, m)), sem((2, n)),
        ]
    scale = (edges * nb * nm) ** (-0.5)
    node = shape((mesh_dev, width), BF16)
    slim_u = shape((nb, width // nb, half), BF16)
    slim_g = shape((nm, width // nm, half), BF16)
    blocks = pltpu.VMEM((2, nm, CAP, half), BF16)
    outs = pl.pallas_call(
        functools.partial(back_kernel, nb, nm, scale),
        out_shape=(node, node, shape((nb, width // nb, width), BF16), slim_u, slim_u, slim_g, slim_g),
        in_specs=[vmem()] * 16,
        out_specs=(vmem(),) * 7,
        scratch_shapes=[
            pltpu.VMEM((nm, CAP, width), BF16), blocks, blocks, blocks,
            pltpu.VMEM((edges, slots_n), BF16), pltpu.VMEM((width, edges), BF16),
            pltpu.VMEM((width, slots_n), BF16), pltpu.VMEM((width, half), F32),
            pltpu.VMEM((width, width), BF16), pltpu.VMEM((2, width, half), BF16),
            pltpu.VMEM((2, width, half), BF16),
            sem((nm,)), sem((nm,)), sem((2, nm)), sem((2, nm)), sem((2, nm)), sem((2, nm)),
        ] + sums,
        compiler_params=params(38, 1),
        name="back",
    )(pick, mesh_latent, cotangent, b_node.reshape(1, -1), local_grid, a_part.reshape(nm, CAP, width),
      s_part.reshape(2, nm, CAP, half), w_edge, w_self, w_agg, w_node_out, u_mesh, slot_col, slope, latent_t,
      rows_in)
    final = shape((width, width), F32)
    return pl.pallas_call(
        write_kernel,
        out_shape=(node, node, final, final, final),
        in_specs=[vmem()] * 7,
        out_specs=(vmem(),) * 5,
        compiler_params=params(16),
        name="write",
    )(*outs[:2], *[o.reshape(width, o.shape[2]) for o in outs[2:]])


def solution(mesh):
    split = P(("band", "mesh"), None)
    flat = P(("band", "mesh"))
    return jax.shard_map(
        functools.partial(shards, mesh.shape["band"], mesh.shape["mesh"]),
        mesh=mesh,
        in_specs=(split, split, split, flat, flat) + (P(),) * 12,
        out_specs=(split, split, P(), P(), P()),
        check_vma=False,
    )
```

```python
import functools

import jax
import jax.numpy as jnp
from jax import lax
from jax.experimental import pallas as pl
from jax.experimental.pallas import tpu as pltpu
from jax.sharding import PartitionSpec as P

CAP = 48
MESH = pl.DeviceIdType.MESH
F32 = jnp.float32
BF16 = jnp.bfloat16
MIB = 1024 * 1024


EB = 512
TB = 256


def sigmoid(v):
    return 0.5 + 0.5 * jnp.tanh(0.5 * v)


def dot(a, b):
    return jnp.dot(a, b, preferred_element_type=F32)


def dot_nt(a, b):
    return lax.dot_general(a, b, (((1,), (1,)), ((), ())), preferred_element_type=F32)


def dot_tn(a, b):
    return lax.dot_general(a, b, (((0,), (0,)), ((), ())), preferred_element_type=F32)


def iota(shape, dim):
    return lax.broadcasted_iota(jnp.int32, shape, dim)


def onehot(mask):
    return jnp.where(mask, 1.0, 0.0).astype(BF16)


def greet(axes):
    barrier = pltpu.get_barrier_semaphore()
    for axis, n in axes:
        me = lax.axis_index(axis)
        for d in range(1, n):
            pl.semaphore_signal(
                barrier, inc=1, device_id={axis: lax.rem(me + d, n)}, device_id_type=MESH
            )


def gathered(axes):
    pl.semaphore_wait(pltpu.get_barrier_semaphore(), sum(n - 1 for _, n in axes))


def send_all(axis, n, src, dst, send_sem, recv_sem):
    me = lax.axis_index(axis)
    copies = []
    for d in range(1, n):
        peer = lax.rem(me + d, n)
        copy = pltpu.make_async_remote_copy(
            src_ref=src(peer),
            dst_ref=dst(me),
            send_sem=send_sem.at[d],
            recv_sem=recv_sem.at[d],
            device_id={axis: peer},
            device_id_type=MESH,
        )
        copy.start()
        copies.append(copy)
    return copies


def wait_all(copies):
    for copy in copies:
        copy.wait()


def columns(rows_ref, out_ref):
    rows = rows_ref.shape[0]
    values = rows_ref[...].astype(F32)
    pad = jnp.zeros((128 - rows, 128), F32)
    turned = jnp.transpose(jnp.concatenate([values, pad], axis=0))
    for r in range(rows):
        out_ref[r * 128 : (r + 1) * 128, :] = jnp.broadcast_to(
            turned[:, r : r + 1], (128, 128)
        ).astype(jnp.int32)


def fetch_kernel(
    nb, nm, em_h, eg_h, gv_h, ml_h, w_in_h, b_in_h, w_out_h, gain_h, u_grid_h, u_mesh_h, b_edge_h,
    table, rows_in, pick, latent_t, pre_grid, slots, slot_col, local_grid, b_edge,
    em, eg, gv, ml, w_in, b_in, w_out, gain, u_grid, u_mesh, load_sem, grid_col, pgrid, left, right, ids_out, ids_in, asked, landed, padded, s1, r1, s2, r2,
):
    mesh_dev = ml.shape[0]
    grid_dev = gv.shape[1]
    rows = em.shape[0]
    me = lax.axis_index("mesh")
    band = lax.axis_index("band")
    loads = []
    for i, (src, dst) in enumerate(
        ((em_h, em), (eg_h, eg), (ml_h, ml), (gv_h, gv), (w_in_h, w_in), (b_in_h, b_in), (w_out_h, w_out),
         (gain_h, gain), (u_grid_h, u_grid), (u_mesh_h, u_mesh), (b_edge_h, b_edge))
    ):
        copy = pltpu.make_async_copy(src, dst, load_sem.at[i])
        copy.start()
        loads.append(copy)
    everyone = (("mesh", nm),)
    greet(everyone)
    loads[0].wait()
    x = em[...] - band * (nm * mesh_dev)
    lane = iota(x.shape, 1)
    row = iota(x.shape, 0)
    prev = pltpu.roll(x, 1, 1)
    prev = jnp.where(lane == 0, pltpu.roll(prev, 1, 0), prev)
    fresh = jnp.where((x != prev) | ((lane == 0) & (row == 0)), 1.0, 0.0)
    fb = fresh.astype(BF16)
    upper = onehot(iota((128, 128), 0) <= iota((128, 128), 1))
    totals = dot(fb, jnp.ones((128, 128), BF16)).astype(BF16)
    lower = onehot(iota((rows, rows), 1) < iota((rows, rows), 0))
    rank = dot(fb, upper) + dot(lower, totals) - 1.0
    owner = jnp.zeros(x.shape, jnp.int32)
    first = jnp.zeros(x.shape, F32)
    for o in range(1, nm):
        later = x >= o * mesh_dev
        begun = jnp.sum(jnp.where(later, 0.0, fresh), keepdims=True)
        owner = owner + jnp.where(later, 1, 0)
        first = jnp.where(later, begun, first)
    inner = (rank - first).astype(jnp.int32)
    slots[...] = owner * CAP + inner
    node = x - owner * mesh_dev
    high = jnp.right_shift(node, 4)
    low = node - high * 16
    high = jnp.where(fresh > 0, high, 0).astype(F32)
    low = jnp.where(fresh > 0, low, 0).astype(F32)
    owner_id = iota((nm, 128), 0)
    inner_id = iota((128, 128), 0)
    for r in range(rows):
        cut = slice(r * 128, (r + 1) * 128)
        mine = owner[r : r + 1, :] == owner_id
        left[0:nm, cut] = jnp.where(mine, high[r : r + 1, :], 0.0).astype(BF16)
        left[nm : 2 * nm, cut] = jnp.where(mine, low[r : r + 1, :], 0.0).astype(BF16)
        right[:, cut] = onehot(inner[r : r + 1, :] == inner_id)
    both = dot_nt(left[...], right[...])
    ids = both[0:nm] * 16.0 + both[nm : 2 * nm]
    for o in range(nm):
        ids_out[o] = jnp.broadcast_to(ids[o : o + 1, :], (8, 128))
    gathered(everyone)
    sent = send_all("mesh", nm, lambda p: ids_out.at[p], lambda q: ids_in.at[q], s1, r1)
    ids_in[me] = ids_out[me]
    for copy in loads[1:3]:
        copy.wait()
    padded[0:mesh_dev, :] = ml[...]
    padded[mesh_dev:, :] = jnp.zeros((padded.shape[0] - mesh_dev, padded.shape[1]), BF16)
    columns(slots, slot_col)
    local_grid[...] = eg[...] - (band * nm + me) * grid_dev
    columns(local_grid, grid_col)
    wait_all(sent)
    turned = jnp.transpose(ids_in[...].reshape(nm * 8, 128))
    for q in range(nm):
        ids_q = jnp.broadcast_to(turned[0:CAP, q * 8 : q * 8 + 1], (CAP, 128)).astype(jnp.int32)
        for t in range(pick.shape[1] // 128):
            pick[q * CAP : (q + 1) * CAP, t * 128 : (t + 1) * 128] = onehot(
                ids_q == iota((CAP, 128), 1) + t * 128
            )
    asked[...] = dot(pick[...], padded[...]).astype(BF16).reshape(asked.shape)
    sent = send_all("mesh", nm, lambda p: asked.at[p], lambda q: landed.at[q], s2, r2)
    landed[me] = asked[me]
    for copy in loads[3:]:
        copy.wait()
    step = 256

    def grid_rows(i, carry):
        cut = pl.ds(pl.multiple_of(i * step, step), step)
        v = dot_tn(gv[:, cut], w_in[...]) + b_in[...]
        hidden = (v * sigmoid(v)).astype(BF16)
        y = dot(hidden, w_out[...])
        centred = y - jnp.mean(y, axis=-1, keepdims=True)
        var = jnp.mean(centred * centred, axis=-1, keepdims=True)
        lat = centred * lax.rsqrt(var + 1e-05) * gain[...]
        latent_t[:, cut] = jnp.transpose(lat).astype(BF16)
        pgrid[cut, :] = dot(lat.astype(BF16), u_grid[...]).astype(BF16)
        return carry

    lax.fori_loop(0, grid_dev // step, grid_rows, 0)

    def grid_edges(b, carry):
        cut = pl.ds(pl.multiple_of(b * EB, EB), EB)
        gcol = grid_col[cut, :]
        hot = jnp.concatenate(
            [onehot(gcol == iota((EB, 128), 1) + t * 128) for t in range(grid_dev // 128)], axis=1
        )
        pre_grid[cut, :] = dot(hot, pgrid[...]).astype(BF16)
        return carry

    lax.fori_loop(0, rows * 128 // EB, grid_edges, 0)
    wait_all(sent)
    rows_in[...] = landed[...].reshape(rows_in.shape)
    table[...] = dot(rows_in[...], u_mesh[...]).astype(BF16)


def edge_kernel(slot_s, slots, slot_col, table, pre_grid, b_edge, a_out, s_out, slope, acc, pre, both):
    rows = slots.shape[0]
    width = table.shape[1]
    tiles = table.shape[0] // TB
    per = EB // 128
    acc[...] = jnp.zeros_like(acc)

    def finish(v):
        s = sigmoid(v)
        act = v * s
        return act.astype(BF16), (s + act * (1.0 - s)).astype(BF16)

    def block(b, carry):
        cut = pl.ds(pl.multiple_of(b * EB, EB), EB)
        low = slot_s[b * per, 0]
        high = slot_s[b * per + per - 1, 127]
        base = pl.multiple_of(jnp.right_shift(low, TB.bit_length() - 1) * TB, TB)
        single = high < base + TB

        @pl.when(single)
        def _():
            window = table[pl.ds(base, TB), :]
            for u in range(per):
                part = pl.ds(pl.multiple_of(b * EB + u * 128, 128), 128)
                scol = slot_col[part, :] - base
                hot = jnp.concatenate([onehot(scol == iota((128, 128), 1) + w * 128) for w in range(TB // 128)], axis=1)
                v = pre_grid[part, :].astype(F32) + b_edge[...] + dot(hot, window)
                act, sl = finish(v)
                both[u * 128 : (u + 1) * 128, 0:width] = act
                both[u * 128 : (u + 1) * 128, width:] = sl
                slope[part, :] = sl
            hot = jnp.concatenate(
                [onehot(slots[pl.ds(b * per + u, 1), :] - base == iota((TB, 128), 0)) for u in range(per)],
                axis=1,
            )
            acc[pl.ds(base, TB), :] += dot(hot, both[...])

        @pl.when(jnp.logical_not(single))
        def _():
            pre[...] = pre_grid[cut, :].astype(F32) + b_edge[...]
            for t in range(tiles):
                @pl.when((low < (t + 1) * TB) & (high >= t * TB))
                def _():
                    scol = slot_col[cut, :]
                    hot = jnp.concatenate(
                        [onehot(scol == iota((EB, 128), 1) + (t * TB + u * 128)) for u in range(TB // 128)],
                        axis=1,
                    )
                    pre[...] += dot(hot, table[t * TB : (t + 1) * TB, :])

            act, sl = finish(pre[...])
            both[:, 0:width] = act
            both[:, width:] = sl
            slope[cut, :] = sl
            for t in range(tiles):
                @pl.when((low < (t + 1) * TB) & (high >= t * TB))
                def _():
                    hot = jnp.concatenate(
                        [onehot(slots[pl.ds(b * per + u, 1), :] == iota((TB, 128), 0) + t * TB) for u in range(per)],
                        axis=1,
                    )
                    acc[t * TB : (t + 1) * TB, :] += dot(hot, both[...])

        return carry

    lax.fori_loop(0, rows // per, block, 0)
    a_out[...] = acc[:, 0:width].astype(BF16)
    half = width // 2
    for c in range(2):
        s_out[c] = acc[:, width + c * half : width + (c + 1) * half].astype(BF16)


def make_sum(nb, nm, scale, out, landed, tot, in1, mid, in2, qp, q1, q2, q3, q4):
    rows = in1.shape[1]
    me = lax.axis_index("mesh")
    band = lax.axis_index("band")
    core = lax.rem(band, 2)
    place = band // 2
    across = nb // 2
    partner = {"band": band + 1 - 2 * core}
    live = {}

    def remote(src, dst, send, recv, device):
        copy = pltpu.make_async_remote_copy(
            src_ref=src, dst_ref=dst, send_sem=send, recv_sem=recv, device_id=device, device_id_type=MESH
        )
        copy.start()
        return copy

    def add(ref, count):
        total = ref[0].astype(F32)
        for q in range(1, count):
            total = total + ref[q].astype(F32)
        return total

    def start(src):
        live[0] = src
        live[1] = remote(src.at[1 - core], landed, qp.at[0], qp.at[1], partner)

    def scatter():
        live[1].wait()
        tot[...] = (live[0][core].astype(F32) + landed[...].astype(F32)).astype(BF16)
        live[2] = send_all(
            "mesh", nm, lambda p: tot.at[pl.ds(pl.multiple_of(p * rows, 16), rows), :],
            lambda q: in1.at[q], q1.at[0], q1.at[1])
        in1[me] = tot[pl.ds(pl.multiple_of(me * rows, 16), rows), :]

    def middle():
        wait_all(live[2])
        mid[...] = add(in1, nm).astype(BF16)
        live[3] = [
            remote(mid, in2.at[place], q2.at[0, d], q2.at[1, d],
                   {"band": lax.rem(place + d, across) * 2 + core})
            for d in range(1, across)
        ]
        in2[place] = mid[...]

    def gather():
        wait_all(live[3])
        out[core, me] = (add(in2, across) * scale).astype(BF16)
        live[4] = send_all("mesh", nm, lambda p: out.at[core, me], lambda q: out.at[core, q], q3.at[0], q3.at[1])
        live[5] = [remote(out.at[core, me], out.at[core, me], q4.at[0, 0], q4.at[1, 0], partner)]

    def forward():
        for d, copy in enumerate(live[4], 1):
            copy.wait_recv()
            part = out.at[core, lax.rem(me + nm - d, nm)]
            live[5].append(remote(part, part, q4.at[0, d], q4.at[1, d], partner))

    def finish():
        for copy in live[4]:
            copy.wait_send()
        wait_all(live[5])

    return start, scatter, middle, gather, forward, finish


GB = 1024


def back_kernel(
    nb, nm, scale, pick, ml, ct, b_node, grid_rows, a_part, s_part, w_edge, w_self, w_agg,
    w_node, u_mesh, slot_col, slope, latent_t, rows_in,
    mesh_out, grad_mesh, oe, o0, o1,
    a_in, s_in, asked, landed, hot_s, lat_e, rows_t, acc, ge, g2,
    sa, ra, ss, rs, sh, rh, *sums,
):
    mesh_dev, width = ml.shape
    half = width // 2
    rows = grid_rows.shape[0]
    slots_n = hot_s.shape[1]
    grid_dev = latent_t.shape[1]
    flat = nm * CAP
    me = lax.axis_index("mesh")
    sum_e, sum_0, sum_1 = [
        make_sum(nb, nm, scale, out, *sums[i * 10 : (i + 1) * 10]) for i, out in enumerate((oe, o0, o1))
    ]

    def send_slopes(c):
        s_in[c, me] = s_part[c, me]
        return send_all("mesh", nm, lambda p: s_part.at[c, p], lambda q: s_in.at[c, q], ss.at[c], rs.at[c])

    everyone = (("mesh", nm), ("band", nb))
    greet(everyone)
    gathered(everyone)
    sent_a = send_all("mesh", nm, lambda p: a_part.at[p], lambda q: a_in.at[q], sa, ra)
    sent_s = [send_slopes(0)]
    a_in[me] = a_part[me]
    own = dot(ml[...], w_self[...]) + b_node[...]
    back = dot_nt(ct[...], w_node[...])

    def build(b, carry):
        cut = pl.ds(pl.multiple_of(b * EB, EB), EB)
        per = EB // 128
        hot = jnp.concatenate(
            [onehot(grid_rows[pl.ds(b * per + u, 1), :] == iota((grid_dev, 128), 0)) for u in range(per)],
            axis=1,
        )
        lat_e[:, cut] = dot(latent_t[...], hot).astype(BF16)
        scol = slot_col[cut, :]
        for t in range(slots_n // 128):
            hot_s[cut, t * 128 : (t + 1) * 128] = onehot(scol == iota((EB, 128), 1) + t * 128)
        return carry

    lax.fori_loop(0, rows * 128 // EB, build, 0)
    rows_t[...] = jnp.transpose(rows_in[...].astype(F32)).astype(BF16)
    wait_all(sent_a)
    acts = dot_tn(pick[...], a_in[...].reshape(flat, width))[0:mesh_dev].astype(BF16)
    agg = dot(acts, w_edge[...]).astype(BF16)
    node_pre = own + dot(agg, w_agg[...])
    s = sigmoid(node_pre)
    node_act = node_pre * s
    g_node = (back * (s + node_act * (1.0 - s))).astype(BF16)
    g_agg = dot_nt(g_node, w_agg[...]).astype(BF16)
    h = dot_nt(g_agg, w_edge[...])
    hb = jnp.concatenate(
        [h.astype(BF16), jnp.zeros((pick.shape[1] - mesh_dev, width), BF16)], axis=0
    )
    sent_h = []
    for c in range(2):
        asked[c] = dot(pick[...], hb[:, c * half : (c + 1) * half]).astype(BF16).reshape(nm, CAP, half)
        sent_h.append(send_all("mesh", nm, lambda p, c=c: asked.at[c, p], lambda q, c=c: landed.at[c, q],
                               sh.at[c], rh.at[c]))
        landed[c, me] = asked[c, me]
    sent_s.append(send_slopes(1))
    g_edge = dot_tn(acts, g_agg).astype(BF16)
    ge[0] = g_edge[:, 0:half]
    ge[1] = g_edge[:, half:]
    sum_e[0](ge)
    mesh_out[...] = (ml[...].astype(F32) + dot(node_act.astype(BF16), w_node[...])).astype(BF16)
    part = ct[...].astype(F32) + dot_nt(g_node, w_self[...])

    def halves(c, between):
        acc[...] = jnp.zeros_like(acc)
        col = slice(c * half, (c + 1) * half)
        wait_all(sent_h[c])
        table = landed[c].reshape(flat, half)
        pm = (table.astype(F32) * s_part[c].reshape(flat, half).astype(F32)).astype(BF16)
        g2[c, 1] = dot(rows_t[...], pm).astype(BF16)
        for b in range(rows * 128 // GB):
            cut = slice(b * GB, (b + 1) * GB)
            g = (dot(hot_s[cut, :], table) * slope[cut, col].astype(F32)).astype(BF16)
            acc[...] += dot(lat_e[:, cut], g)
            if b in between:
                between[b]()
        g2[c, 0] = acc[...].astype(BF16)

    last = rows * 128 // GB - 1
    sum_e[1]()
    halves(0, {})
    sum_0[0](g2.at[0])
    halves(1, {min(1, last): sum_0[1]})
    sum_1[0](g2.at[1])
    wait_all(sent_s[0])
    wait_all(sent_s[1])
    slopes = jnp.concatenate(
        [dot_tn(pick[...], s_in[c].reshape(flat, half))[0:mesh_dev] for c in range(2)], axis=1
    )
    sum_1[1]()
    sum_e[2]()
    g_pmesh = (h * slopes).astype(BF16)
    grad_mesh[...] = (part + dot_nt(g_pmesh, u_mesh[...])).astype(BF16)
    sum_e[3]()
    sum_0[2]()
    sum_0[3]()
    sum_1[2]()
    sum_1[3]()
    sum_e[4]()
    sum_0[4]()
    sum_1[4]()
    sum_e[5]()
    sum_0[5]()
    sum_1[5]()


def write_kernel(mo, gm, e, g0, g1, mo_out, gm_out, e_out, g_out, u_out):
    half = e.shape[2]
    mo_out[...] = mo[...]
    gm_out[...] = gm[...]
    for c, both in enumerate((g0, g1)):
        col = slice(c * half, (c + 1) * half)
        e_out[:, col] = e[c].astype(F32)
        g_out[:, col] = both[0].astype(F32)
        u_out[:, col] = both[1].astype(F32)


def vmem():
    return pl.BlockSpec(memory_space=pltpu.VMEM)


def shape(dims, kind):
    return jax.ShapeDtypeStruct(dims, kind)


def params(mib, cid=None):
    if cid is None:
        return pltpu.CompilerParams(vmem_limit_bytes=mib * MIB)
    return pltpu.CompilerParams(
        vmem_limit_bytes=mib * MIB, collective_id=cid, has_side_effects=True
    )


def shards(
    nb, nm, grid_vars, mesh_latent, cotangent, edge_grid, edge_mesh, w_in, b_in, w_out, norm_gain,
    u_grid, u_mesh, b_edge, w_edge, w_self, w_agg, b_node, w_node_out,
):
    grid_dev = grid_vars.shape[0]
    mesh_dev, width = mesh_latent.shape
    edges = edge_grid.shape[0]
    rows = edges // 128
    slots_n = nm * CAP
    padded = -(-mesh_dev // 128) * 128
    sem = pltpu.SemaphoreType.DMA
    em = edge_mesh.reshape(rows, 128)
    eg = edge_grid.reshape(rows, 128)
    table, rows_in, pick, latent_t, pre_grid, slots, slot_col, local_grid, bias = pl.pallas_call(
        functools.partial(fetch_kernel, nb, nm),
        out_shape=(
            shape((slots_n, width), BF16), shape((slots_n, width), BF16), shape((slots_n, padded), BF16),
            shape((width, grid_dev), BF16), shape((edges, width), BF16),
            shape((rows, 128), jnp.int32), shape((edges, 128), jnp.int32), shape((rows, 128), jnp.int32),
            shape((1, width), F32),
        ),
        in_specs=[pl.BlockSpec(memory_space=pltpu.HBM)] * 11,
        out_specs=(vmem(),) * 9,
        scratch_shapes=[
            pltpu.VMEM((rows, 128), jnp.int32), pltpu.VMEM((rows, 128), jnp.int32),
            pltpu.VMEM((grid_vars.shape[1], grid_dev), BF16), pltpu.VMEM((mesh_dev, width), BF16),
            pltpu.VMEM((grid_vars.shape[1], width), BF16), pltpu.VMEM((1, width), F32),
            pltpu.VMEM((width, width), BF16), pltpu.VMEM((1, width), F32),
            pltpu.VMEM((width, width), BF16), pltpu.VMEM((width, width), BF16), sem((11,)),
            pltpu.VMEM((edges, 128), jnp.int32), pltpu.VMEM((grid_dev, width), BF16),
            pltpu.VMEM((2 * nm, edges), BF16), pltpu.VMEM((128, edges), BF16),
            pltpu.VMEM((nm, 8, 128), F32), pltpu.VMEM((nm, 8, 128), F32),
            pltpu.VMEM((nm, CAP, width), BF16), pltpu.VMEM((nm, CAP, width), BF16),
            pltpu.VMEM((padded, width), BF16),
            sem((nm,)), sem((nm,)), sem((nm,)), sem((nm,)),
        ],
        compiler_params=params(24, 0),
        name="fetch",
    )(*[
        pltpu.with_memory_space_constraint(v, pltpu.HBM)
        for v in (em, eg, grid_vars.T, mesh_latent, w_in, b_in.reshape(1, -1), w_out,
                  norm_gain.reshape(1, -1), u_grid, u_mesh, b_edge.reshape(1, -1))
    ])
    half = width // 2
    a_part, s_part, slope = pl.pallas_call(
        edge_kernel,
        out_shape=(
            shape((slots_n, width), BF16), shape((2, slots_n, half), BF16), shape((edges, width), BF16),
        ),
        in_specs=[pl.BlockSpec(memory_space=pltpu.SMEM)] + [vmem()] * 5,
        out_specs=(vmem(),) * 3,
        scratch_shapes=[
            pltpu.VMEM((slots_n, 2 * width), F32), pltpu.VMEM((EB, width), F32),
            pltpu.VMEM((EB, 2 * width), BF16),
        ],
        compiler_params=params(16),
        name="edges",
    )(slots, slots, slot_col, table, pre_grid, bias)
    part = width // nm
    sums = [
        pltpu.VMEM((width, half), BF16), pltpu.VMEM((width, half), BF16), pltpu.VMEM((nm, part, half), BF16),
        pltpu.VMEM((part, half), BF16), pltpu.VMEM((nb // 2, part, half), BF16),
        sem((2,)), sem((2, nm)), sem((2, nb)), sem((2, nm)), sem((2, nm)),
    ] * 3
    scale = (edges * nb * nm) ** (-0.5)
    node = shape((mesh_dev, width), BF16)
    summed = shape((2, nm, part, half), BF16)
    blocks = pltpu.VMEM((2, nm, CAP, half), BF16)
    outs = pl.pallas_call(
        functools.partial(back_kernel, nb, nm, scale),
        out_shape=(node, node, summed, summed, summed),
        in_specs=[vmem()] * 16,
        out_specs=(vmem(),) * 5,
        scratch_shapes=[
            pltpu.VMEM((nm, CAP, width), BF16), blocks, blocks, blocks,
            pltpu.VMEM((edges, slots_n), BF16), pltpu.VMEM((width, edges), BF16),
            pltpu.VMEM((width, slots_n), BF16), pltpu.VMEM((width, half), F32),
            pltpu.VMEM((2, width, half), BF16), pltpu.VMEM((2, 2, width, half), BF16),
            sem((nm,)), sem((nm,)), sem((2, nm)), sem((2, nm)), sem((2, nm)), sem((2, nm)),
        ] + sums,
        compiler_params=params(38, 1),
        name="back",
    )(pick, mesh_latent, cotangent, b_node.reshape(1, -1), local_grid, a_part.reshape(nm, CAP, width),
      s_part.reshape(2, nm, CAP, half), w_edge, w_self, w_agg, w_node_out, u_mesh, slot_col, slope, latent_t,
      rows_in)
    final = shape((width, width), F32)
    return pl.pallas_call(
        write_kernel,
        out_shape=(node, node, final, final, final),
        in_specs=[vmem()] * 5,
        out_specs=(vmem(),) * 5,
        compiler_params=params(16),
        name="write",
    )(*outs[:2], *[o.reshape(2, width, half) for o in outs[2:]])


def solution(mesh):
    split = P(("band", "mesh"), None)
    flat = P(("band", "mesh"))
    return jax.shard_map(
        functools.partial(shards, mesh.shape["band"], mesh.shape["mesh"]),
        mesh=mesh,
        in_specs=(split, split, split, flat, flat) + (P(),) * 12,
        out_specs=(split, split, P(), P(), P()),
        check_vma=False,
    )
```

```python
import functools

import jax
import jax.numpy as jnp
from jax import lax
from jax.experimental import pallas as pl
from jax.experimental.pallas import tpu as pltpu
from jax.sharding import PartitionSpec as P

CAP = 48
MESH = pl.DeviceIdType.MESH
F32 = jnp.float32
BF16 = jnp.bfloat16
MIB = 1024 * 1024


EB = 512
TB = 256


def sigmoid(v):
    return 0.5 + 0.5 * jnp.tanh(0.5 * v)


def dot(a, b):
    return jnp.dot(a, b, preferred_element_type=F32)


def dot_nt(a, b):
    return lax.dot_general(a, b, (((1,), (1,)), ((), ())), preferred_element_type=F32)


def dot_tn(a, b):
    return lax.dot_general(a, b, (((0,), (0,)), ((), ())), preferred_element_type=F32)


def iota(shape, dim):
    return lax.broadcasted_iota(jnp.int32, shape, dim)


def onehot(mask):
    return jnp.where(mask, 1.0, 0.0).astype(BF16)


def greet(axes):
    barrier = pltpu.get_barrier_semaphore()
    for axis, n in axes:
        me = lax.axis_index(axis)
        for d in range(1, n):
            pl.semaphore_signal(
                barrier, inc=1, device_id={axis: lax.rem(me + d, n)}, device_id_type=MESH
            )


def gathered(axes):
    pl.semaphore_wait(pltpu.get_barrier_semaphore(), sum(n - 1 for _, n in axes))


def send_all(axis, n, src, dst, send_sem, recv_sem):
    me = lax.axis_index(axis)
    copies = []
    for d in range(1, n):
        peer = lax.rem(me + d, n)
        copy = pltpu.make_async_remote_copy(
            src_ref=src(peer),
            dst_ref=dst(me),
            send_sem=send_sem.at[d],
            recv_sem=recv_sem.at[d],
            device_id={axis: peer},
            device_id_type=MESH,
        )
        copy.start()
        copies.append(copy)
    return copies


def wait_all(copies):
    for copy in copies:
        copy.wait()


def columns(rows_ref, out_ref):
    rows = rows_ref.shape[0]
    values = rows_ref[...].astype(F32)
    pad = jnp.zeros((128 - rows, 128), F32)
    turned = jnp.transpose(jnp.concatenate([values, pad], axis=0))
    for r in range(rows):
        out_ref[r * 128 : (r + 1) * 128, :] = jnp.broadcast_to(
            turned[:, r : r + 1], (128, 128)
        ).astype(jnp.int32)


def fetch_kernel(
    nb, nm, em_h, eg_h, gv_h, ml_h, w_in_h, b_in_h, w_out_h, gain_h, u_grid_h, u_mesh_h, b_edge_h,
    table, rows_in, pick, latent_t, pre_grid, slots, slot_col, local_grid, b_edge,
    em, eg, gv, ml, w_in, b_in, w_out, gain, u_grid, u_mesh, load_sem, grid_col, pgrid, left, right, ids_out, ids_in, asked, landed, padded, s1, r1, s2, r2,
):
    mesh_dev = ml.shape[0]
    grid_dev = gv.shape[1]
    rows = em.shape[0]
    me = lax.axis_index("mesh")
    band = lax.axis_index("band")
    loads = []
    for i, (src, dst) in enumerate(
        ((em_h, em), (eg_h, eg), (ml_h, ml), (gv_h, gv), (w_in_h, w_in), (b_in_h, b_in), (w_out_h, w_out),
         (gain_h, gain), (u_grid_h, u_grid), (u_mesh_h, u_mesh), (b_edge_h, b_edge))
    ):
        copy = pltpu.make_async_copy(src, dst, load_sem.at[i])
        copy.start()
        loads.append(copy)
    everyone = (("mesh", nm),)
    greet(everyone)
    loads[0].wait()
    x = em[...] - band * (nm * mesh_dev)
    lane = iota(x.shape, 1)
    row = iota(x.shape, 0)
    prev = pltpu.roll(x, 1, 1)
    prev = jnp.where(lane == 0, pltpu.roll(prev, 1, 0), prev)
    fresh = jnp.where((x != prev) | ((lane == 0) & (row == 0)), 1.0, 0.0)
    fb = fresh.astype(BF16)
    upper = onehot(iota((128, 128), 0) <= iota((128, 128), 1))
    totals = dot(fb, jnp.ones((128, 128), BF16)).astype(BF16)
    lower = onehot(iota((rows, rows), 1) < iota((rows, rows), 0))
    rank = dot(fb, upper) + dot(lower, totals) - 1.0
    owner = jnp.zeros(x.shape, jnp.int32)
    first = jnp.zeros(x.shape, F32)
    for o in range(1, nm):
        later = x >= o * mesh_dev
        begun = jnp.sum(jnp.where(later, 0.0, fresh), keepdims=True)
        owner = owner + jnp.where(later, 1, 0)
        first = jnp.where(later, begun, first)
    inner = (rank - first).astype(jnp.int32)
    slots[...] = owner * CAP + inner
    node = x - owner * mesh_dev
    high = jnp.right_shift(node, 4)
    low = node - high * 16
    high = jnp.where(fresh > 0, high, 0).astype(F32)
    low = jnp.where(fresh > 0, low, 0).astype(F32)
    owner_id = iota((nm, 128), 0)
    inner_id = iota((128, 128), 0)
    for r in range(rows):
        cut = slice(r * 128, (r + 1) * 128)
        mine = owner[r : r + 1, :] == owner_id
        left[0:nm, cut] = jnp.where(mine, high[r : r + 1, :], 0.0).astype(BF16)
        left[nm : 2 * nm, cut] = jnp.where(mine, low[r : r + 1, :], 0.0).astype(BF16)
        right[:, cut] = onehot(inner[r : r + 1, :] == inner_id)
    both = dot_nt(left[...], right[...])
    ids = both[0:nm] * 16.0 + both[nm : 2 * nm]
    for o in range(nm):
        ids_out[o] = jnp.broadcast_to(ids[o : o + 1, :], (8, 128))
    gathered(everyone)
    sent = send_all("mesh", nm, lambda p: ids_out.at[p], lambda q: ids_in.at[q], s1, r1)
    ids_in[me] = ids_out[me]
    for copy in loads[1:3]:
        copy.wait()
    padded[0:mesh_dev, :] = ml[...]
    padded[mesh_dev:, :] = jnp.zeros((padded.shape[0] - mesh_dev, padded.shape[1]), BF16)
    columns(slots, slot_col)
    local_grid[...] = eg[...] - (band * nm + me) * grid_dev
    columns(local_grid, grid_col)
    wait_all(sent)
    turned = jnp.transpose(ids_in[...].reshape(nm * 8, 128))
    for q in range(nm):
        ids_q = jnp.broadcast_to(turned[0:CAP, q * 8 : q * 8 + 1], (CAP, 128)).astype(jnp.int32)
        for t in range(pick.shape[1] // 128):
            pick[q * CAP : (q + 1) * CAP, t * 128 : (t + 1) * 128] = onehot(
                ids_q == iota((CAP, 128), 1) + t * 128
            )
    asked[...] = dot(pick[...], padded[...]).astype(BF16).reshape(asked.shape)
    sent = send_all("mesh", nm, lambda p: asked.at[p], lambda q: landed.at[q], s2, r2)
    landed[me] = asked[me]
    for copy in loads[3:]:
        copy.wait()
    step = 256

    def grid_rows(i, carry):
        cut = pl.ds(pl.multiple_of(i * step, step), step)
        v = dot_tn(gv[:, cut], w_in[...]) + b_in[...]
        hidden = (v * sigmoid(v)).astype(BF16)
        y = dot(hidden, w_out[...])
        centred = y - jnp.mean(y, axis=-1, keepdims=True)
        var = jnp.mean(centred * centred, axis=-1, keepdims=True)
        lat = centred * lax.rsqrt(var + 1e-05) * gain[...]
        latent_t[:, cut] = jnp.transpose(lat).astype(BF16)
        pgrid[cut, :] = dot(lat.astype(BF16), u_grid[...]).astype(BF16)
        return carry

    lax.fori_loop(0, grid_dev // step, grid_rows, 0)

    def grid_edges(b, carry):
        cut = pl.ds(pl.multiple_of(b * EB, EB), EB)
        gcol = grid_col[cut, :]
        hot = jnp.concatenate(
            [onehot(gcol == iota((EB, 128), 1) + t * 128) for t in range(grid_dev // 128)], axis=1
        )
        pre_grid[cut, :] = dot(hot, pgrid[...]).astype(BF16)
        return carry

    lax.fori_loop(0, rows * 128 // EB, grid_edges, 0)
    wait_all(sent)
    rows_in[...] = landed[...].reshape(rows_in.shape)
    table[...] = dot(rows_in[...], u_mesh[...]).astype(BF16)


def edge_kernel(slot_s, slots, slot_col, table, pre_grid, b_edge, a_out, s_out, slope, acc, pre, both):
    rows = slots.shape[0]
    width = table.shape[1]
    tiles = table.shape[0] // TB
    per = EB // 128
    acc[...] = jnp.zeros_like(acc)

    def finish(v):
        s = sigmoid(v)
        act = v * s
        return act.astype(BF16), (s + act * (1.0 - s)).astype(BF16)

    def block(b, carry):
        cut = pl.ds(pl.multiple_of(b * EB, EB), EB)
        low = slot_s[b * per, 0]
        high = slot_s[b * per + per - 1, 127]
        base = pl.multiple_of(jnp.right_shift(low, TB.bit_length() - 1) * TB, TB)
        single = high < base + TB

        @pl.when(single)
        def _():
            window = table[pl.ds(base, TB), :]
            for u in range(per):
                part = pl.ds(pl.multiple_of(b * EB + u * 128, 128), 128)
                scol = slot_col[part, :] - base
                hot = jnp.concatenate([onehot(scol == iota((128, 128), 1) + w * 128) for w in range(TB // 128)], axis=1)
                v = pre_grid[part, :].astype(F32) + b_edge[...] + dot(hot, window)
                act, sl = finish(v)
                both[u * 128 : (u + 1) * 128, 0:width] = act
                both[u * 128 : (u + 1) * 128, width:] = sl
                slope[part, :] = sl
            hot = jnp.concatenate(
                [onehot(slots[pl.ds(b * per + u, 1), :] - base == iota((TB, 128), 0)) for u in range(per)],
                axis=1,
            )
            acc[pl.ds(base, TB), :] += dot(hot, both[...])

        @pl.when(jnp.logical_not(single))
        def _():
            pre[...] = pre_grid[cut, :].astype(F32) + b_edge[...]
            for t in range(tiles):
                @pl.when((low < (t + 1) * TB) & (high >= t * TB))
                def _():
                    scol = slot_col[cut, :]
                    hot = jnp.concatenate(
                        [onehot(scol == iota((EB, 128), 1) + (t * TB + u * 128)) for u in range(TB // 128)],
                        axis=1,
                    )
                    pre[...] += dot(hot, table[t * TB : (t + 1) * TB, :])

            act, sl = finish(pre[...])
            both[:, 0:width] = act
            both[:, width:] = sl
            slope[cut, :] = sl
            for t in range(tiles):
                @pl.when((low < (t + 1) * TB) & (high >= t * TB))
                def _():
                    hot = jnp.concatenate(
                        [onehot(slots[pl.ds(b * per + u, 1), :] == iota((TB, 128), 0) + t * TB) for u in range(per)],
                        axis=1,
                    )
                    acc[t * TB : (t + 1) * TB, :] += dot(hot, both[...])

        return carry

    lax.fori_loop(0, rows // per, block, 0)
    a_out[...] = acc[:, 0:width].astype(BF16)
    half = width // 2
    for c in range(2):
        s_out[c] = acc[:, width + c * half : width + (c + 1) * half].astype(BF16)


def make_sum(nb, nm, scale, out, landed, tot, in1, mid, in2, qp, q1, q2, q3, q4):
    rows = in1.shape[1]
    me = lax.axis_index("mesh")
    band = lax.axis_index("band")
    core = lax.rem(band, 2)
    place = band // 2
    across = nb // 2
    partner = {"band": band + 1 - 2 * core}
    live = {}

    def remote(src, dst, send, recv, device):
        copy = pltpu.make_async_remote_copy(
            src_ref=src, dst_ref=dst, send_sem=send, recv_sem=recv, device_id=device, device_id_type=MESH
        )
        copy.start()
        return copy

    def add(ref, count):
        total = ref[0].astype(F32)
        for q in range(1, count):
            total = total + ref[q].astype(F32)
        return total

    def start(src):
        live[0] = src
        live[1] = remote(src.at[1 - core], landed, qp.at[0], qp.at[1], partner)

    def scatter():
        live[1].wait()
        tot[...] = (live[0][core].astype(F32) + landed[...].astype(F32)).astype(BF16)
        live[2] = send_all(
            "mesh", nm, lambda p: tot.at[pl.ds(pl.multiple_of(p * rows, 16), rows), :],
            lambda q: in1.at[q], q1.at[0], q1.at[1])
        in1[me] = tot[pl.ds(pl.multiple_of(me * rows, 16), rows), :]

    def middle():
        wait_all(live[2])
        mid[...] = add(in1, nm).astype(BF16)
        live[3] = [
            remote(mid, in2.at[place], q2.at[0, d], q2.at[1, d],
                   {"band": lax.rem(place + d, across) * 2 + core})
            for d in range(1, across)
        ]
        in2[place] = mid[...]

    def gather():
        wait_all(live[3])
        out[core, me] = (add(in2, across) * scale).astype(BF16)
        live[4] = send_all("mesh", nm, lambda p: out.at[core, me], lambda q: out.at[core, q], q3.at[0], q3.at[1])
        live[5] = [remote(out.at[core, me], out.at[core, me], q4.at[0, 0], q4.at[1, 0], partner)]

    def forward():
        for d, copy in enumerate(live[4], 1):
            copy.wait_recv()
            part = out.at[core, lax.rem(me + nm - d, nm)]
            live[5].append(remote(part, part, q4.at[0, d], q4.at[1, d], partner))

    def finish():
        for copy in live[4]:
            copy.wait_send()
        wait_all(live[5])

    return start, scatter, middle, gather, forward, finish


GB = 1024


def back_kernel(
    nb, nm, scale, pick, ml, ct, b_node, grid_rows, a_part, s_part, w_edge, w_self, w_agg,
    w_node, u_mesh, slot_col, slope, latent_t, rows_in,
    mesh_out, grad_mesh, oe, o0, o1,
    a_in, s_in, asked, landed, hot_s, lat_e, rows_t, acc, ge, g2,
    sa, ra, ss, rs, sh, rh, *sums,
):
    mesh_dev, width = ml.shape
    half = width // 2
    rows = grid_rows.shape[0]
    slots_n = hot_s.shape[1]
    grid_dev = latent_t.shape[1]
    flat = nm * CAP
    me = lax.axis_index("mesh")
    sum_e, sum_0, sum_1 = [
        make_sum(nb, nm, scale, out, *sums[i * 10 : (i + 1) * 10]) for i, out in enumerate((oe, o0, o1))
    ]

    def send_slopes(c):
        s_in[c, me] = s_part[c, me]
        return send_all("mesh", nm, lambda p: s_part.at[c, p], lambda q: s_in.at[c, q], ss.at[c], rs.at[c])

    everyone = (("mesh", nm), ("band", nb))
    greet(everyone)
    gathered(everyone)
    sent_a = send_all("mesh", nm, lambda p: a_part.at[p], lambda q: a_in.at[q], sa, ra)
    sent_s = [send_slopes(0)]
    a_in[me] = a_part[me]
    own = dot(ml[...], w_self[...]) + b_node[...]
    back = dot_nt(ct[...], w_node[...])

    def build(b, carry):
        cut = pl.ds(pl.multiple_of(b * EB, EB), EB)
        per = EB // 128
        hot = jnp.concatenate(
            [onehot(grid_rows[pl.ds(b * per + u, 1), :] == iota((grid_dev, 128), 0)) for u in range(per)],
            axis=1,
        )
        lat_e[:, cut] = dot(latent_t[...], hot).astype(BF16)
        scol = slot_col[cut, :]
        for t in range(slots_n // 128):
            hot_s[cut, t * 128 : (t + 1) * 128] = onehot(scol == iota((EB, 128), 1) + t * 128)
        return carry

    lax.fori_loop(0, rows * 128 // EB, build, 0)
    rows_t[...] = jnp.transpose(rows_in[...].astype(F32)).astype(BF16)
    wait_all(sent_a)
    acts = dot_tn(pick[...], a_in[...].reshape(flat, width))[0:mesh_dev].astype(BF16)
    agg = dot(acts, w_edge[...]).astype(BF16)
    node_pre = own + dot(agg, w_agg[...])
    s = sigmoid(node_pre)
    node_act = node_pre * s
    g_node = (back * (s + node_act * (1.0 - s))).astype(BF16)
    g_agg = dot_nt(g_node, w_agg[...]).astype(BF16)
    h = dot_nt(g_agg, w_edge[...])
    hb = jnp.concatenate(
        [h.astype(BF16), jnp.zeros((pick.shape[1] - mesh_dev, width), BF16)], axis=0
    )
    sent_h = []
    for c in range(2):
        asked[c] = dot(pick[...], hb[:, c * half : (c + 1) * half]).astype(BF16).reshape(nm, CAP, half)
        sent_h.append(send_all("mesh", nm, lambda p, c=c: asked.at[c, p], lambda q, c=c: landed.at[c, q],
                               sh.at[c], rh.at[c]))
        landed[c, me] = asked[c, me]
    sent_s.append(send_slopes(1))
    g_edge = dot_tn(acts, g_agg).astype(BF16)
    ge[0] = g_edge[:, 0:half]
    ge[1] = g_edge[:, half:]
    sum_e[0](ge)
    mesh_out[...] = (ml[...].astype(F32) + dot(node_act.astype(BF16), w_node[...])).astype(BF16)
    part = ct[...].astype(F32) + dot_nt(g_node, w_self[...])

    def halves(c, between):
        acc[...] = jnp.zeros_like(acc)
        col = slice(c * half, (c + 1) * half)
        wait_all(sent_h[c])
        table = landed[c].reshape(flat, half)
        pm = (table.astype(F32) * s_part[c].reshape(flat, half).astype(F32)).astype(BF16)
        g2[c, 1] = dot(rows_t[...], pm).astype(BF16)
        for b in range(rows * 128 // GB):
            cut = slice(b * GB, (b + 1) * GB)
            g = (dot(hot_s[cut, :], table) * slope[cut, col].astype(F32)).astype(BF16)
            acc[...] += dot(lat_e[:, cut], g)
            if b in between:
                between[b]()
        g2[c, 0] = acc[...].astype(BF16)

    last = rows * 128 // GB - 1
    sum_e[1]()
    halves(0, {})
    sum_0[0](g2.at[0])
    halves(1, {min(1, last): sum_0[1]})
    sum_1[0](g2.at[1])
    wait_all(sent_s[0])
    wait_all(sent_s[1])
    slopes = jnp.concatenate(
        [dot_tn(pick[...], s_in[c].reshape(flat, half))[0:mesh_dev] for c in range(2)], axis=1
    )
    sum_1[1]()
    sum_0[2]()
    sum_e[2]()
    g_pmesh = (h * slopes).astype(BF16)
    grad_mesh[...] = (part + dot_nt(g_pmesh, u_mesh[...])).astype(BF16)
    sum_0[3]()
    sum_e[3]()
    sum_1[2]()
    sum_1[3]()
    sum_e[4]()
    sum_0[4]()
    sum_1[4]()
    sum_e[5]()
    sum_0[5]()
    sum_1[5]()


def write_kernel(mo, gm, e, g0, g1, mo_out, gm_out, e_out, g_out, u_out):
    half = e.shape[2]
    mo_out[...] = mo[...]
    gm_out[...] = gm[...]
    for c, both in enumerate((g0, g1)):
        col = slice(c * half, (c + 1) * half)
        e_out[:, col] = e[c].astype(F32)
        g_out[:, col] = both[0].astype(F32)
        u_out[:, col] = both[1].astype(F32)


def vmem():
    return pl.BlockSpec(memory_space=pltpu.VMEM)


def shape(dims, kind):
    return jax.ShapeDtypeStruct(dims, kind)


def params(mib, cid=None):
    if cid is None:
        return pltpu.CompilerParams(vmem_limit_bytes=mib * MIB)
    return pltpu.CompilerParams(
        vmem_limit_bytes=mib * MIB, collective_id=cid, has_side_effects=True
    )


def shards(
    nb, nm, grid_vars, mesh_latent, cotangent, edge_grid, edge_mesh, w_in, b_in, w_out, norm_gain,
    u_grid, u_mesh, b_edge, w_edge, w_self, w_agg, b_node, w_node_out,
):
    grid_dev = grid_vars.shape[0]
    mesh_dev, width = mesh_latent.shape
    edges = edge_grid.shape[0]
    rows = edges // 128
    slots_n = nm * CAP
    padded = -(-mesh_dev // 128) * 128
    sem = pltpu.SemaphoreType.DMA
    em = edge_mesh.reshape(rows, 128)
    eg = edge_grid.reshape(rows, 128)
    table, rows_in, pick, latent_t, pre_grid, slots, slot_col, local_grid, bias = pl.pallas_call(
        functools.partial(fetch_kernel, nb, nm),
        out_shape=(
            shape((slots_n, width), BF16), shape((slots_n, width), BF16), shape((slots_n, padded), BF16),
            shape((width, grid_dev), BF16), shape((edges, width), BF16),
            shape((rows, 128), jnp.int32), shape((edges, 128), jnp.int32), shape((rows, 128), jnp.int32),
            shape((1, width), F32),
        ),
        in_specs=[pl.BlockSpec(memory_space=pltpu.HBM)] * 11,
        out_specs=(vmem(),) * 9,
        scratch_shapes=[
            pltpu.VMEM((rows, 128), jnp.int32), pltpu.VMEM((rows, 128), jnp.int32),
            pltpu.VMEM((grid_vars.shape[1], grid_dev), BF16), pltpu.VMEM((mesh_dev, width), BF16),
            pltpu.VMEM((grid_vars.shape[1], width), BF16), pltpu.VMEM((1, width), F32),
            pltpu.VMEM((width, width), BF16), pltpu.VMEM((1, width), F32),
            pltpu.VMEM((width, width), BF16), pltpu.VMEM((width, width), BF16), sem((11,)),
            pltpu.VMEM((edges, 128), jnp.int32), pltpu.VMEM((grid_dev, width), BF16),
            pltpu.VMEM((2 * nm, edges), BF16), pltpu.VMEM((128, edges), BF16),
            pltpu.VMEM((nm, 8, 128), F32), pltpu.VMEM((nm, 8, 128), F32),
            pltpu.VMEM((nm, CAP, width), BF16), pltpu.VMEM((nm, CAP, width), BF16),
            pltpu.VMEM((padded, width), BF16),
            sem((nm,)), sem((nm,)), sem((nm,)), sem((nm,)),
        ],
        compiler_params=params(24, 0),
        name="fetch",
    )(*[
        pltpu.with_memory_space_constraint(v, pltpu.HBM)
        for v in (em, eg, grid_vars.T, mesh_latent, w_in, b_in.reshape(1, -1), w_out,
                  norm_gain.reshape(1, -1), u_grid, u_mesh, b_edge.reshape(1, -1))
    ])
    half = width // 2
    a_part, s_part, slope = pl.pallas_call(
        edge_kernel,
        out_shape=(
            shape((slots_n, width), BF16), shape((2, slots_n, half), BF16), shape((edges, width), BF16),
        ),
        in_specs=[pl.BlockSpec(memory_space=pltpu.SMEM)] + [vmem()] * 5,
        out_specs=(vmem(),) * 3,
        scratch_shapes=[
            pltpu.VMEM((slots_n, 2 * width), F32), pltpu.VMEM((EB, width), F32),
            pltpu.VMEM((EB, 2 * width), BF16),
        ],
        compiler_params=params(16),
        name="edges",
    )(slots, slots, slot_col, table, pre_grid, bias)
    part = width // nm
    sums = [
        pltpu.VMEM((width, half), BF16), pltpu.VMEM((width, half), BF16), pltpu.VMEM((nm, part, half), BF16),
        pltpu.VMEM((part, half), BF16), pltpu.VMEM((nb // 2, part, half), BF16),
        sem((2,)), sem((2, nm)), sem((2, nb)), sem((2, nm)), sem((2, nm)),
    ] * 3
    scale = (edges * nb * nm) ** (-0.5)
    node = shape((mesh_dev, width), BF16)
    summed = shape((2, nm, part, half), BF16)
    blocks = pltpu.VMEM((2, nm, CAP, half), BF16)
    outs = pl.pallas_call(
        functools.partial(back_kernel, nb, nm, scale),
        out_shape=(node, node, summed, summed, summed),
        in_specs=[vmem()] * 16,
        out_specs=(vmem(),) * 5,
        scratch_shapes=[
            pltpu.VMEM((nm, CAP, width), BF16), blocks, blocks, blocks,
            pltpu.VMEM((edges, slots_n), BF16), pltpu.VMEM((width, edges), BF16),
            pltpu.VMEM((width, slots_n), BF16), pltpu.VMEM((width, half), F32),
            pltpu.VMEM((2, width, half), BF16), pltpu.VMEM((2, 2, width, half), BF16),
            sem((nm,)), sem((nm,)), sem((2, nm)), sem((2, nm)), sem((2, nm)), sem((2, nm)),
        ] + sums,
        compiler_params=params(38, 1),
        name="back",
    )(pick, mesh_latent, cotangent, b_node.reshape(1, -1), local_grid, a_part.reshape(nm, CAP, width),
      s_part.reshape(2, nm, CAP, half), w_edge, w_self, w_agg, w_node_out, u_mesh, slot_col, slope, latent_t,
      rows_in)
    final = shape((width, width), F32)
    return pl.pallas_call(
        write_kernel,
        out_shape=(node, node, final, final, final),
        in_specs=[vmem()] * 5,
        out_specs=(vmem(),) * 5,
        compiler_params=params(16),
        name="write",
    )(*outs[:2], *[o.reshape(2, width, half) for o in outs[2:]])


def solution(mesh):
    split = P(("band", "mesh"), None)
    flat = P(("band", "mesh"))
    return jax.shard_map(
        functools.partial(shards, mesh.shape["band"], mesh.shape["mesh"]),
        mesh=mesh,
        in_specs=(split, split, split, flat, flat) + (P(),) * 12,
        out_specs=(split, split, P(), P(), P()),
        check_vma=False,
    )
```
